32 devices in a mesh: gx: 4 (over z), gy: 8 (over y, x, core).
Axes of the slice: x: 2, y: 2, z: 4, core: 2. Of those that a mesh axis runs over, the one named last changes fastest.
Arguments:
- residual_in: float32 [3, 32, 64, 128], P(None, 'gx', 'gy'), may hold values from -24 to 24, as said below
- accumulation: float32 [3, 3, 32, 64, 128], P(None, None, 'gx', 'gy'), may hold values from -2.4 to 8, as said below
- mobility: float32 [3, 3, 32, 64, 128], P(None, None, 'gx', 'gy'), may hold values from -0.9 to 3, as said below
- permeability: float32 [3, 32, 64, 128], P(None, 'gx', 'gy'), may hold values from 0.1 to 10
- fault_near: int32 [4, 8, 1024], P('gx', 'gy'), may hold values from 0 to 8191, as said below
- fault_far: int32 [4, 8, 1024], P('gx', 'gy'), may hold values from 0 to 8191, as said below
- fault_trans: float32 [4, 8, 1024], P('gx', 'gy'), may hold values from 0 to 5, as said below
- well_cells: int32 [4, 8, 2], P('gx', 'gy'), may hold values from 0 to 8191
- well_rates: float32 [4, 8, 2], P('gx', 'gy'), may hold values from 1 to 5
Outputs:
- newton_update: float32 [3, 32, 64, 128], P(None, 'gx', 'gy')
- decoupled_residual: float32 [3, 32, 64, 128], P(None, 'gx', 'gy')
The draws below stay inside these ranges and needn't reach their ends.
Inputs may be any that keep to these rules, and one draw needn't show every extreme that they name: `accumulation`: each row's off-diagonal entries together are at most 0.6 times its positive diagonal entry. `mobility`: each row's off-diagonal entries together are at most 0.6 times its positive diagonal entry. `fault_near`: a local index of a cell in the last two rows along the second areal dimension of its device's block. `fault_far`: a local index of a cell in the first two rows along the second areal dimension of its device's block. `fault_trans`: at each boundary the live slots come first and the rest are zero; all slots of devices with j = 0 are zero; some boundary uses all 1024 slots. `residual_in`: values at most 24 in magnitude. `well_cells`: a local index of a cell of its device's block.
All inputs are finite; a program needn't handle non-finite values.
Results may differ from the reference program's by a relative error of at most 0.0012.
Values sent between devices are 32-bit elements; how exact they have to be, the bound alone decides.
A program may use at most 64 MiB of HBM per device.

```python
import math
import jax
import jax.numpy as jnp
from jax import lax

CX = 8
CY = 8
NZ = 128
FCAP = 1024
WELLS = 2
KRYLOV = 3
BLOCKS_X = 4
BLOCKS_Y = 8
NX = 32
NY = 64
N_GX = 4
N_GY = 8


def draw_residual_in(key, part):
    shape_full = (3, NX, NY, NZ)
    noise_key, scale_key = jax.random.split(key)
    rough = jnp.exp(jax.random.uniform(scale_key, shape_full, jnp.float32, jnp.log(0.5), jnp.log(2.0)))
    ramp = 1.0 + 2.0 * jnp.arange(NY, dtype=jnp.float32) / max(NY - 1, 1)
    base = jnp.clip(jax.random.normal(noise_key, shape_full, jnp.float32), -4.0, 4.0)
    return base * rough * ramp[None, None, :, None]


def dominant_blocks(key, low, high):
    diag_key, off_key = jax.random.split(key)
    diag_values = jnp.exp(jax.random.uniform(diag_key, (3, NX, NY, NZ), jnp.float32, jnp.log(low), jnp.log(high)))
    off_values = jax.random.uniform(off_key, (3, 3, NX, NY, NZ), jnp.float32, -0.3, 0.3)
    identity = (jnp.arange(3)[:, None] == jnp.arange(3)[None, :])[:, :, None, None, None]
    return jnp.where(identity, diag_values[:, None], diag_values[:, None] * off_values)


def draw_accumulation(key, part):
    return dominant_blocks(key, 0.5, 5.0)


def draw_mobility(key, part):
    return dominant_blocks(key, 0.5, 2.0)


def fault_cells(key, top_rows):
    column_key, row_key, layer_key = jax.random.split(key, 3)
    shape_full = (NX // CX, NY // CY, FCAP)
    columns = jax.random.randint(column_key, shape_full, 0, CX)
    rows_off = jax.random.randint(row_key, shape_full, 0, 2)
    layers = jax.random.randint(layer_key, shape_full, 0, NZ)
    if top_rows:
        rows_at = CY - 1 - rows_off
    else:
        rows_at = rows_off
    return ((columns * CY + rows_at) * NZ + layers).astype(jnp.int32)


def draw_fault_near(key, part):
    return fault_cells(jax.random.fold_in(key, 11), True)


def draw_fault_far(key, part):
    return fault_cells(jax.random.fold_in(key, 12), False)


def draw_fault_trans(key, part):
    blocks_x = NX // CX
    blocks_y = NY // CY
    divisor = jax.random.randint(jax.random.fold_in(key, 7), (blocks_x, blocks_y), 1, 5)
    counts = FCAP // divisor
    chosen = jax.random.randint(jax.random.fold_in(key, 8), (), 0, blocks_x * (blocks_y - 1))
    counts = counts.at[chosen // (blocks_y - 1), chosen % (blocks_y - 1) + 1].set(FCAP)
    slots = jnp.arange(FCAP)[None, None, :]
    live = (slots < counts[:, :, None]) & (jnp.arange(blocks_y)[None, :, None] >= 1)
    value_key = jax.random.fold_in(key, 9)
    values = jnp.exp(jax.random.uniform(value_key, (blocks_x, blocks_y, FCAP), jnp.float32, jnp.log(0.5), jnp.log(5.0)))
    return jnp.where(live, values, 0.0)


def set_ends(entries, stream_key, least, largest):
    longest = entries.shape.index(max(entries.shape))
    spots = []
    for shift in (0, 1):
        where = [jax.random.randint(jax.random.fold_in(stream_key, axis), (), 0, length) for axis, length in enumerate(entries.shape)]
        where[longest] = (where[longest] + shift) % entries.shape[longest]
        spots.append(tuple(where))
    return entries.at[spots[0]].set(least).at[spots[1]].set(largest)


def block_levels(own_key, shape, pieces, low, high):
    factor_of, own = 1.0, jax.random.fold_in(own_key, 6)
    for position, blocks in pieces:
        draws = jnp.exp(jax.random.uniform(jax.random.fold_in(own, position), (blocks,), jnp.float32, low / len(pieces), high / len(pieces)))
        factor_of = factor_of * jnp.repeat(draws, shape[position] // blocks).reshape([-1 if axis == position else 1 for axis in range(len(shape))])
    return factor_of


def setup_inputs(seed: int = 0) -> dict:
    key_list = jax.random.split(jax.random.key(seed), 10)
    residual_in = draw_residual_in(jax.random.fold_in(key_list[9], 71), 0)
    accumulation = draw_accumulation(jax.random.fold_in(key_list[9], 71), 0)
    mobility = draw_mobility(jax.random.fold_in(key_list[9], 71), 0)
    permeability = jnp.clip(jnp.exp(math.log(10.0) - 4.6051702 * jax.random.uniform(key_list[3], (3, NX, NY, NZ), jnp.float32) ** block_levels(key_list[3], (3, NX, NY, NZ), ((1, 4), (2, 8)), -0.2, 0.2)), 0.1, 10.0)
    fault_near = draw_fault_near(jax.random.fold_in(key_list[9], 71), 0)
    fault_far = draw_fault_far(jax.random.fold_in(key_list[9], 71), 0)
    fault_trans = draw_fault_trans(jax.random.fold_in(key_list[9], 71), 0)
    well_cells = set_ends(jax.random.randint(key_list[7], (BLOCKS_X, BLOCKS_Y, WELLS), 0, CX * CY * NZ), jax.random.fold_in(key_list[7], 1), 0, (CX * CY * NZ) - 1).astype(jnp.int32)
    well_rates = jnp.clip(jnp.exp(math.log(5.0) - 1.609438 * jax.random.uniform(key_list[8], (BLOCKS_X, BLOCKS_Y, WELLS), jnp.float32) ** block_levels(key_list[8], (BLOCKS_X, BLOCKS_Y, WELLS), ((0, 4), (1, 8)), -0.2, 0.2)), 1.0, 5.0)
    return dict(residual_in=residual_in, accumulation=accumulation, mobility=mobility, permeability=permeability, fault_near=fault_near, fault_far=fault_far, fault_trans=fault_trans, well_cells=well_cells, well_rates=well_rates)


def harmonic(first_perm, second_perm):
    return 2.0 * first_perm * second_perm / (first_perm + second_perm)

def apply_blocks(blocks, vector):
    return lax.optimization_barrier(jnp.sum(blocks * vector[None], axis=1))

def invert_blocks(blocks):

    def part(row_one, col_one, row_two, col_two):
        return blocks[row_one, col_one] * blocks[row_two, col_two] - blocks[row_one, col_two] * blocks[row_two, col_one]
    cofactor = [[part(1, 1, 2, 2), -part(1, 0, 2, 2), part(1, 0, 2, 1)], [-part(0, 1, 2, 2), part(0, 0, 2, 2), -part(0, 0, 2, 1)], [part(0, 1, 1, 2), -part(0, 0, 1, 2), part(0, 0, 1, 1)]]
    determinant = blocks[0, 0] * cofactor[0][0] + blocks[0, 1] * cofactor[0][1] + blocks[0, 2] * cofactor[0][2]
    return jnp.stack([jnp.stack([cofactor[inner][outer] for inner in range(3)]) for outer in range(3)]) / determinant

def solve_small(matrix, rhs_values):
    size_count = len(rhs_values)
    matrix_rows = [list(line) for line in matrix]
    values = list(rhs_values)
    for column in range(size_count):
        for lower in range(column + 1, size_count):
            factor = matrix_rows[lower][column] / matrix_rows[column][column]
            matrix_rows[lower] = [entry - factor * pivot for entry, pivot in zip(matrix_rows[lower], matrix_rows[column])]
            values[lower] = values[lower] - factor * values[column]
    solved = [0.0] * size_count
    for column in reversed(range(size_count)):
        partial_sum = values[column]
        for later in range(column + 1, size_count):
            partial_sum = partial_sum - matrix_rows[column][later] * solved[later]
        solved[column] = partial_sum / matrix_rows[column][column]
    return solved

def global_index(local):
    column = local // (CY * NZ)
    row_in = local // NZ % CY
    layer = local % NZ
    block_x = jnp.arange(N_GX, dtype=jnp.int32)[:, None, None]
    block_y = jnp.arange(N_GY, dtype=jnp.int32)[None, :, None]
    return (((block_x * CX + column) * NY + block_y * CY + row_in) * NZ + layer).astype(jnp.int32)

def reference(residual_in, accumulation, mobility, permeability, fault_near, fault_far, fault_trans, well_cells, well_rates):
    perm_x, perm_y, perm_z = (permeability[0], permeability[1], permeability[2])
    pad_x = jnp.pad(perm_x, ((1, 1), (0, 0), (0, 0)))
    pad_y = jnp.pad(perm_y, ((0, 0), (1, 1), (0, 0)))
    pad_z = jnp.pad(perm_z, ((0, 0), (0, 0), (1, 1)))
    trans_east = harmonic(perm_x, pad_x[2:])
    trans_west = harmonic(perm_x, pad_x[:-2])
    trans_north = harmonic(perm_y, pad_y[:, 2:])
    trans_south = harmonic(perm_y, pad_y[:, :-2])
    trans_above = harmonic(perm_z, pad_z[:, :, 2:])
    trans_below = harmonic(perm_z, pad_z[:, :, :-2])
    near_global = global_index(fault_near)[:, :-1].reshape(-1)
    far_global = global_index(fault_far)[:, 1:].reshape(-1)
    pair_trans = fault_trans[:, 1:].reshape(-1)
    totals = trans_east + trans_west + trans_north + trans_south + trans_above + trans_below
    totals = totals.reshape(-1).at[far_global].add(pair_trans).at[near_global].add(pair_trans).reshape(NX, NY, NZ)
    diagonal = accumulation + totals[None, None] * mobility
    weight_one = diagonal[0, 1] / diagonal[1, 1]
    weight_two = diagonal[0, 2] / diagonal[2, 2]
    decoupled_block = jnp.stack([diagonal[0] - weight_one * diagonal[1] - weight_two * diagonal[2], diagonal[1], diagonal[2]])
    inverse = invert_blocks(decoupled_block)

    def decouple(vector):
        return jnp.stack([vector[0] - weight_one * vector[1] - weight_two * vector[2], vector[1], vector[2]])

    def jacobian(vector):
        flux_in = apply_blocks(mobility, vector)
        padded = jnp.pad(flux_in, ((0, 0), (1, 1), (1, 1), (1, 1)))
        result = apply_blocks(accumulation, vector)
        result = result + trans_east * (flux_in - padded[:, 2:, 1:-1, 1:-1])
        result = result + trans_west * (flux_in - padded[:, :-2, 1:-1, 1:-1])
        result = result + trans_north * (flux_in - padded[:, 1:-1, 2:, 1:-1])
        result = result + trans_south * (flux_in - padded[:, 1:-1, :-2, 1:-1])
        result = result + trans_above * (flux_in - padded[:, 1:-1, 1:-1, 2:])
        result = result + trans_below * (flux_in - padded[:, 1:-1, 1:-1, :-2])
        flat_flux = flux_in.reshape(3, -1)
        pair_flux = pair_trans * (flat_flux[:, far_global] - flat_flux[:, near_global])
        flat_result = result.reshape(3, -1).at[:, far_global].add(pair_flux).at[:, near_global].add(-pair_flux)
        return decouple(flat_result.reshape(result.shape))
    well_global = global_index(well_cells).reshape(-1)
    rhs = (-residual_in).reshape(3, -1).at[1, well_global].add(well_rates.reshape(-1)).reshape(residual_in.shape)
    bprime = decouple(rhs)
    norm_rhs = jnp.sqrt(jnp.sum(bprime * bprime))
    basis = [bprime / norm_rhs]
    directions = []
    hessen = [[0.0] * KRYLOV for row_index in range(KRYLOV + 1)]
    for iteration in range(KRYLOV):
        direction = apply_blocks(inverse, basis[iteration])
        image = jacobian(direction)
        directions.append(direction)
        for earlier in range(iteration + 1):
            coeff = jnp.sum(image * basis[earlier])
            hessen[earlier][iteration] = coeff
            image = image - coeff * basis[earlier]
        subdiag = jnp.sqrt(jnp.sum(image * image))
        hessen[iteration + 1][iteration] = subdiag
        basis.append(image / subdiag)
    normal = [[sum((hessen[row_index][left] * hessen[row_index][right] for row_index in range(KRYLOV + 1))) for right in range(KRYLOV)] for left in range(KRYLOV)]
    small_rhs = [norm_rhs * hessen[0][left] for left in range(KRYLOV)]
    coefs = solve_small(normal, small_rhs)
    update = coefs[0] * directions[0]
    for iteration in range(1, KRYLOV):
        update = update + coefs[iteration] * directions[iteration]
    return (update, bprime - jacobian(update))
```

```python
import functools

import jax
import jax.numpy as jnp
from jax import lax
from jax.experimental import pallas as pl
from jax.experimental.pallas import tpu as pltpu
from jax.sharding import PartitionSpec as P

KRYLOV = 3
PAIRS = [(a, b) for a in range(KRYLOV + 1) for b in range(a, KRYLOV + 1)]
MESH = pl.DeviceIdType.MESH


def harmonic(a, b):
    return 2.0 * a * b / (a + b)


def quotient(value, by):
    if by & (by - 1) == 0:
        return lax.shift_right_logical(value, jnp.int32(by.bit_length() - 1))
    return value // by


def split_two(value):
    high = value.astype(jnp.bfloat16)
    low = (value - high.astype(jnp.float32)).astype(jnp.bfloat16)
    return high, low


def solve_small(matrix, rhs_values):
    size = len(rhs_values)
    rows = [list(line) for line in matrix]
    values = list(rhs_values)
    for column in range(size):
        for lower in range(column + 1, size):
            factor = rows[lower][column] / rows[column][column]
            rows[lower] = [e - factor * p for e, p in zip(rows[lower], rows[column])]
            values[lower] = values[lower] - factor * values[column]
    solved = [0.0] * size
    for column in reversed(range(size)):
        partial = values[column]
        for later in range(column + 1, size):
            partial = partial - rows[column][later] * solved[later]
        solved[column] = partial / rows[column][column]
    return solved


def kernel(
    nx, ny, cx, cy, nz, cap, wells,
    res_h, acc_h, mob_h, perm_h, near_h, far_h, tr_h, wc_ref, wr_ref,
    upd_o, out_o,
    res_v, acc_v, mob_v, perm_v, near_v, far_v, tr_v,
    far_u, tr_u, near_l,
    ps_u, ps_l, py_l, py_u, px_l, px_u,
    tot, inv, mix, w_v, ys, flux, offs,
    send_u, send_l, send_e, send_w, recv_l, recv_u, recv_w, recv_e,
    z_far, z_near, z_near_l, z_far_u,
    red_y, red_x,
    load_sem, s0, r0, s1, r1, sy, ry, sx, rx,
):
    gx, gy = lax.axis_index("gx"), lax.axis_index("gy")
    has_l, has_u = gy > 0, gy < ny - 1
    has_w, has_e = gx > 0, gx < nx - 1

    barrier = pltpu.get_barrier_semaphore()
    for d in range(1, ny):
        pl.semaphore_signal(barrier, inc=1, device_id={"gy": lax.rem(gy + d, ny)}, device_id_type=MESH)
    for d in range(1, nx):
        pl.semaphore_signal(barrier, inc=1, device_id={"gx": lax.rem(gx + d, nx)}, device_id_type=MESH)

    loads = []
    for k, (src, dst) in enumerate([
        (perm_h, perm_v), (near_h, near_v), (far_h, far_v), (tr_h, tr_v),
        (acc_h, acc_v), (mob_h, mob_v), (res_h, res_v),
    ]):
        copy = pltpu.make_async_copy(src, dst, load_sem.at[k])
        copy.start()
        loads.append(copy)

    loads[0].wait()
    perm = perm_v.reshape(3 * cx * cy, nz)
    ps_u[...] = perm[pl.ds(cx * cy + cy - 1, cx, stride=cy), :]
    ps_l[...] = perm[pl.ds(cx * cy, cx, stride=cy), :]
    for k in (1, 2, 3):
        loads[k].wait()

    pl.semaphore_wait(barrier, nx + ny - 2)

    def remote(src, dst, send, recv, target):
        return pltpu.make_async_remote_copy(
            src_ref=src, dst_ref=dst, send_sem=send, recv_sem=recv,
            device_id=target, device_id_type=MESH,
        )

    up, down = {"gy": gy + 1}, {"gy": gy - 1}
    east, west = {"gx": gx + 1}, {"gx": gx - 1}
    first_u = [
        remote(near_v, near_l, s0.at[0], r0.at[0], up),
        remote(ps_u, py_l, s0.at[1], r0.at[1], up),
    ]
    first_l = [
        remote(far_v, far_u, s0.at[2], r0.at[2], down),
        remote(tr_v, tr_u, s0.at[3], r0.at[3], down),
        remote(ps_l, py_u, s0.at[4], r0.at[4], down),
    ]
    first_e = [remote(perm_v.at[0, cx - 1], px_l, s0.at[5], r0.at[5], east)]
    first_w = [remote(perm_v.at[0, 0], px_u, s0.at[6], r0.at[6], west)]

    def start(to_u, to_l, to_e, to_w):
        for flag, copies in ((has_u, to_u), (has_l, to_l), (has_e, to_e), (has_w, to_w)):
            @pl.when(flag)
            def _(copies=copies):
                for copy in copies:
                    copy.start()

    def arrive(to_u, to_l, to_e, to_w):
        for flag, copies in ((has_u, to_l), (has_l, to_u), (has_e, to_w), (has_w, to_e)):
            @pl.when(flag)
            def _(copies=copies):
                for copy in copies:
                    copy.wait_recv()

    def sent(to_u, to_l, to_e, to_w):
        for flag, copies in ((has_u, to_u), (has_l, to_l), (has_e, to_e), (has_w, to_w)):
            @pl.when(flag)
            def _(copies=copies):
                for copy in copies:
                    copy.wait_send()

    start(first_u, first_l, first_e, first_w)

    def clear(flag, *refs):
        @pl.when(jnp.logical_not(flag))
        def _():
            for ref in refs:
                ref[...] = jnp.zeros(ref.shape, ref.dtype)

    clear(has_l, near_l, py_l, recv_l)
    clear(has_u, far_u, tr_u, py_u, recv_u)
    clear(has_w, px_l, recv_w)
    clear(has_e, px_u, recv_e)

    rows = 2 * cx
    row_iota = lax.broadcasted_iota(jnp.int32, (rows, cap), 0)
    layer_iota = lax.broadcasted_iota(jnp.int32, (nz, cap), 0)

    def slots(ref, base, onehot):
        index = ref[...]
        column = quotient(index, nz)
        layer = index - column * nz
        across = quotient(column, cy)
        along = column - across * cy - base
        onehot[...] = jnp.where(layer_iota == layer, 1.0, 0.0).astype(jnp.bfloat16)
        return row_iota == along * cx + across

    far_rows = slots(far_v, 0, z_far)
    near_rows = slots(near_v, cy - 2, z_near)

    def scatter(values, where_rows, onehot):
        parts = []
        for value in values:
            chosen = jnp.where(where_rows, value, 0.0)
            parts.extend(split_two(chosen))
        spread = lax.dot_general(
            jnp.concatenate(parts, axis=0), onehot[...], (((1,), (1,)), ((), ())),
            preferred_element_type=jnp.float32,
        )
        return [
            spread[2 * c * rows:(2 * c + 1) * rows] + spread[(2 * c + 1) * rows:(2 * c + 2) * rows]
            for c in range(len(values))
        ]

    def gather(block, where_rows, onehot):
        high, low = split_two(block)
        found = lax.dot_general(
            jnp.concatenate([high, low], axis=0), onehot[...], (((1,), (0,)), ((), ())),
            preferred_element_type=jnp.float32,
        )
        found = found[:3 * rows] + found[3 * rows:]
        return [
            jnp.sum(jnp.where(where_rows, found[c * rows:(c + 1) * rows], 0.0), axis=0, keepdims=True)
            for c in range(3)
        ]

    trans = tr_v[...]
    perm_x, perm_y, perm_z = perm_v[0], perm_v[1], perm_v[2]
    y_iota = lax.broadcasted_iota(jnp.int32, (cx, cy, nz), 1)
    z_iota = lax.broadcasted_iota(jnp.int32, (cx, cy, nz), 2)
    t_x = harmonic(perm_x[:-1], perm_x[1:])
    t_n = jnp.where(y_iota == cy - 1, 0.0, harmonic(perm_y, pltpu.roll(perm_y, cy - 1, 1)))
    t_s = jnp.where(y_iota == 0, 0.0, harmonic(perm_y, pltpu.roll(perm_y, 1, 1)))
    t_a = jnp.where(z_iota == nz - 1, 0.0, harmonic(perm_z, pltpu.roll(perm_z, nz - 1, 2)))
    t_b = jnp.where(z_iota == 0, 0.0, harmonic(perm_z, pltpu.roll(perm_z, 1, 2)))
    far_sum = scatter([trans], far_rows, z_far)[0]

    arrive(first_u, first_l, first_e, first_w)
    near_rows_l = slots(near_l, cy - 2, z_near_l)
    far_rows_u = slots(far_u, 0, z_far_u)
    trans_u = tr_u[...]
    near_sum = scatter([trans_u], near_rows, z_near)[0]
    t_w0 = harmonic(perm_x[0], px_l[...])
    t_e1 = harmonic(perm_x[cx - 1], px_u[...])
    t_e = jnp.concatenate([t_x, t_e1[None]], axis=0)
    t_w = jnp.concatenate([t_w0[None], t_x], axis=0)
    t_s0 = harmonic(ps_l[...], py_l[...])
    t_n1 = harmonic(ps_u[...], py_u[...])

    flat = cx * cy
    tot[...] = (t_e + t_w + t_n + t_s + t_a + t_b).reshape(flat, nz)

    def add_rows(ref, start_row, value):
        place = (pl.ds(start_row, cx, stride=cy), slice(None))
        ref[place] = ref[place] + value

    add_rows(tot, 0, far_sum[:cx] + t_s0)
    add_rows(tot, 1, far_sum[cx:])
    add_rows(tot, cy - 2, near_sum[:cx])
    add_rows(tot, cy - 1, near_sum[cx:] + t_n1)

    for k in (4, 5, 6):
        loads[k].wait()
    total = tot[...].reshape(cx, cy, nz)
    mob = [[mob_v[a, b] for b in range(3)] for a in range(3)]
    diag = [[acc_v[a, b] + total * mob[a][b] for b in range(3)] for a in range(3)]
    w1 = diag[0][1] / diag[1][1]
    w2 = diag[0][2] / diag[2][2]
    w_v[0] = w1
    w_v[1] = w2
    blk = [[diag[0][b] - w1 * diag[1][b] - w2 * diag[2][b] for b in range(3)], diag[1], diag[2]]

    def part(a, b, c, d):
        return blk[a][b] * blk[c][d] - blk[a][d] * blk[c][b]

    cof = [
        [part(1, 1, 2, 2), -part(1, 0, 2, 2), part(1, 0, 2, 1)],
        [-part(0, 1, 2, 2), part(0, 0, 2, 2), -part(0, 0, 2, 1)],
        [part(0, 1, 1, 2), -part(0, 0, 1, 2), part(0, 0, 1, 1)],
    ]
    det = blk[0][0] * cof[0][0] + blk[0][1] * cof[0][1] + blk[0][2] * cof[0][2]
    inverse_det = 1.0 / det
    pre = [[cof[b][a] * inverse_det for b in range(3)] for a in range(3)]
    for a in range(3):
        for b in range(3):
            inv[a, b] = pre[a][b]
            mix[a, b] = mob[a][0] * pre[0][b] + mob[a][1] * pre[1][b] + mob[a][2] * pre[2][b]

    lin = (
        lax.broadcasted_iota(jnp.int32, (cx, cy, nz), 0) * (cy * nz) + y_iota * nz + z_iota
    )
    rhs0, rhs1, rhs2 = -res_v[0], -res_v[1], -res_v[2]
    for w in range(wells):
        rhs1 = rhs1 + jnp.where(lin == wc_ref[0, w], wr_ref[0, w], 0.0)
    ys[0, 0] = rhs0 - w1 * rhs1 - w2 * rhs2
    ys[0, 1] = rhs1
    ys[0, 2] = rhs2

    pending = [(first_u, first_l, first_e, first_w)]
    for it in range(KRYLOV):
        y = [ys[it, c] for c in range(3)]
        field = []
        for a in range(3):
            value = mix[a, 0] * y[0] + mix[a, 1] * y[1] + mix[a, 2] * y[2]
            field.append(value)
            flux[pl.ds(a * flat, flat), :] = value.reshape(flat, nz)
            send_e[it, a] = value[cx - 1]
            send_w[it, a] = value[0]
        for a in range(3):
            for r in range(2):
                at = pl.ds((2 * a + r) * cx, cx)
                send_u[it, at, :] = flux[pl.ds(a * flat + cy - 2 + r, cx, stride=cy), :]
                send_l[it, at, :] = flux[pl.ds(a * flat + r, cx, stride=cy), :]
        copies = (
            [remote(send_u.at[it], recv_l.at[it], s1.at[it, 0], r1.at[it, 0], up)],
            [remote(send_l.at[it], recv_u.at[it], s1.at[it, 1], r1.at[it, 1], down)],
            [remote(send_e.at[it], recv_w.at[it], s1.at[it, 2], r1.at[it, 2], east)],
            [remote(send_w.at[it], recv_e.at[it], s1.at[it, 3], r1.at[it, 3], west)],
        )
        start(*copies)
        pending.append(copies)
        inner = []
        for a in range(3):
            f = field[a]
            near_sums = (
                t_n * pltpu.roll(f, cy - 1, 1) + t_s * pltpu.roll(f, 1, 1)
                + t_a * pltpu.roll(f, nz - 1, 2) + t_b * pltpu.roll(f, 1, 2)
            )
            inner.append(near_sums)
        arrive(*copies)
        below, above = recv_l[it], recv_u[it]
        got_l = gather(below, near_rows_l, z_near_l)
        got_u = gather(above, far_rows_u, z_far_u)
        fault_l = scatter([trans * g for g in got_l], far_rows, z_far)
        fault_u = scatter([trans_u * g for g in got_u], near_rows, z_near)
        for a in range(3):
            f = field[a]
            value = (
                inner[a]
                + t_e * jnp.concatenate([f[1:], recv_e[it, a][None]], axis=0)
                + t_w * jnp.concatenate([recv_w[it, a][None], f[:-1]], axis=0)
            )
            offs[pl.ds(a * flat, flat), :] = value.reshape(flat, nz)
            halo_s = below[(2 * a + 1) * cx:(2 * a + 2) * cx]
            halo_n = above[2 * a * cx:(2 * a + 1) * cx]
            add_rows(offs, a * flat, fault_l[a][:cx] + t_s0 * halo_s)
            add_rows(offs, a * flat + 1, fault_l[a][cx:])
            add_rows(offs, a * flat + cy - 2, fault_u[a][:cx])
            add_rows(offs, a * flat + cy - 1, fault_u[a][cx:] + t_n1 * halo_n)
        o = [offs[pl.ds(a * flat, flat), :].reshape(cx, cy, nz) for a in range(3)]
        ys[it + 1, 0] = y[0] - (o[0] - w_v[0] * o[1] - w_v[1] * o[2])
        ys[it + 1, 1] = y[1] - o[1]
        ys[it + 1, 2] = y[2] - o[2]

    count = red_y.shape[1]
    lines = []
    for left, right in PAIRS:
        lines.append(
            jnp.sum(jnp.sum(ys[left] * ys[right], axis=(0, 1)), axis=0, keepdims=True)
        )
    lines.append(jnp.zeros((count - len(PAIRS), nz), jnp.float32))
    red_y[gy] = jnp.concatenate(lines, axis=0)
    around = [
        remote(red_y.at[gy], red_y.at[gy], sy.at[d], ry.at[d], {"gy": lax.rem(gy + d, ny)})
        for d in range(1, ny)
    ]
    for copy in around:
        copy.start()
    for copy in around:
        copy.wait_recv()
    partial = red_y[0]
    for d in range(1, ny):
        partial = partial + red_y[d]
    red_x[gx] = partial
    across = [
        remote(red_x.at[gx], red_x.at[gx], sx.at[d], rx.at[d], {"gx": lax.rem(gx + d, nx)})
        for d in range(1, nx)
    ]
    for copy in across:
        copy.start()
    for copy in across:
        copy.wait_recv()
    partial = red_x[0]
    for d in range(1, nx):
        partial = partial + red_x[d]
    sums = jnp.broadcast_to(jnp.sum(partial, axis=1, keepdims=True), partial.shape)

    def entry(left, right):
        k = PAIRS.index((min(left, right), max(left, right)))
        return sums[k:k + 1]

    normal = [[entry(a + 1, b + 1) for b in range(KRYLOV)] for a in range(KRYLOV)]
    coefs = solve_small(normal, [entry(0, a + 1) for a in range(KRYLOV)])
    coefs = [c.reshape(1, 1, nz) for c in coefs]
    mixed = []
    for c in range(3):
        combined = coefs[0] * ys[0, c]
        applied = coefs[0] * ys[1, c]
        for k in range(1, KRYLOV):
            combined = combined + coefs[k] * ys[k, c]
            applied = applied + coefs[k] * ys[k + 1, c]
        mixed.append(combined)
        out_o[c] = ys[0, c] - applied
    for c in range(3):
        upd_o[c] = inv[c, 0] * mixed[0] + inv[c, 1] * mixed[1] + inv[c, 2] * mixed[2]
    for group in pending:
        sent(*group)
    for copy in around + across:
        copy.wait_send()


def solution(mesh):
    nx, ny = mesh.shape["gx"], mesh.shape["gy"]
    placed = (
        P(None, "gx", "gy", None),
        P(None, None, "gx", "gy", None),
        P(None, None, "gx", "gy", None),
        P(None, "gx", "gy", None),
    ) + (P("gx", "gy", None),) * 5

    def shards(residual_in, accumulation, mobility, permeability, fault_near, fault_far, fault_trans, well_cells, well_rates):
        _, cx, cy, nz = residual_in.shape
        cap = fault_near.shape[-1]
        wells = well_cells.shape[-1]
        flat = cx * cy
        lines = -(-len(PAIRS) // 8) * 8
        f32, i32, bf16 = jnp.float32, jnp.int32, jnp.bfloat16
        vm = pltpu.VMEM
        dma = pltpu.SemaphoreType.DMA
        scratch = [
            vm((3, cx, cy, nz), f32), vm((3, 3, cx, cy, nz), f32), vm((3, 3, cx, cy, nz), f32),
            vm((3, cx, cy, nz), f32),
            vm((1, cap), i32), vm((1, cap), i32), vm((1, cap), f32),
            vm((1, cap), i32), vm((1, cap), f32), vm((1, cap), i32),
        ]
        scratch += [vm((cx, nz), f32)] * 4 + [vm((cy, nz), f32)] * 2
        scratch += [
            vm((flat, nz), f32), vm((3, 3, cx, cy, nz), f32), vm((3, 3, cx, cy, nz), f32),
            vm((2, cx, cy, nz), f32), vm((KRYLOV + 1, 3, cx, cy, nz), f32),
            vm((3 * flat, nz), f32), vm((3 * flat, nz), f32),
        ]
        scratch += [vm((KRYLOV, 6 * cx, nz), f32)] * 2 + [vm((KRYLOV, 3, cy, nz), f32)] * 2
        scratch += [vm((KRYLOV, 6 * cx, nz), f32)] * 2 + [vm((KRYLOV, 3, cy, nz), f32)] * 2
        scratch += [vm((nz, cap), bf16)] * 4
        scratch += [vm((ny, lines, nz), f32), vm((nx, lines, nz), f32)]
        scratch += [
            dma((7,)), dma((7,)), dma((7,)), dma((KRYLOV, 4)), dma((KRYLOV, 4)),
            dma((ny,)), dma((ny,)), dma((nx,)), dma((nx,)),
        ]
        anywhere = pl.BlockSpec(memory_space=pl.ANY)
        scalars = pl.BlockSpec(memory_space=pltpu.SMEM)
        inside = pl.BlockSpec(memory_space=pltpu.VMEM)
        shape = jax.ShapeDtypeStruct(residual_in.shape, f32)
        return pl.pallas_call(
            functools.partial(kernel, nx, ny, cx, cy, nz, cap, wells),
            out_shape=(shape, shape),
            in_specs=[anywhere] * 7 + [scalars] * 2,
            out_specs=(inside, inside),
            scratch_shapes=scratch,
            compiler_params=pltpu.CompilerParams(collective_id=0, has_side_effects=True),
            name="newton",
        )(
            residual_in, accumulation, mobility, permeability,
            fault_near.reshape(1, cap), fault_far.reshape(1, cap), fault_trans.reshape(1, cap),
            well_cells.reshape(1, wells), well_rates.reshape(1, wells),
        )

    out = P(None, "gx", "gy", None)
    return jax.shard_map(shards, mesh=mesh, in_specs=placed, out_specs=(out, out), check_vma=False)
```

```python
import functools

import jax
import jax.numpy as jnp
from jax import lax
from jax.experimental import pallas as pl
from jax.experimental.pallas import tpu as pltpu
from jax.sharding import PartitionSpec as P

KRYLOV = 3
PAIRS = [(a, b) for b in range(KRYLOV + 1) for a in range(b + 1)]
MESH = pl.DeviceIdType.MESH


def harmonic(a, b):
    return 2.0 * a * b / (a + b)


def quotient(value, by):
    if by & (by - 1) == 0:
        return lax.shift_right_logical(value, jnp.int32(by.bit_length() - 1))
    return value // by


def split_two(value):
    high = value.astype(jnp.bfloat16)
    low = (value - high.astype(jnp.float32)).astype(jnp.bfloat16)
    return high, low


def solve_small(matrix, rhs_values):
    size = len(rhs_values)
    rows = [list(line) for line in matrix]
    values = list(rhs_values)
    for column in range(size):
        for lower in range(column + 1, size):
            factor = rows[lower][column] / rows[column][column]
            rows[lower] = [e - factor * p for e, p in zip(rows[lower], rows[column])]
            values[lower] = values[lower] - factor * values[column]
    solved = [0.0] * size
    for column in reversed(range(size)):
        partial = values[column]
        for later in range(column + 1, size):
            partial = partial - rows[column][later] * solved[later]
        solved[column] = partial / rows[column][column]
    return solved


def kernel(
    nx, ny, cx, cy, nz, cap, wells, direct,
    res_h, acc_h, mob_h, perm_h, near_h, far_h, tr_h, wc_h, wr_h,
    upd_o, out_o,
    res_v, acc_v, mob_v, perm_v, near_v, far_v, tr_v,
    wc_ref, wr_ref,
    far_u, tr_u, near_l,
    ps_u, ps_l, py_l, py_u, px_l, px_u,
    tot, inv, mix, w_v, ys, flux, offs,
    send_u, send_l, send_e, send_w, recv_l, recv_u, recv_w, recv_e,
    z_far, z_near, z_near_l, z_far_u,
    red_y, red_x,
    load_sem, s0, r0, s1, r1, sy, ry, sx, rx,
):
    gx, gy = lax.axis_index("gx"), lax.axis_index("gy")
    has_l, has_u = gy > 0, gy < ny - 1
    has_w, has_e = gx > 0, gx < nx - 1

    barrier = pltpu.get_barrier_semaphore()
    for d in range(1, ny):
        pl.semaphore_signal(barrier, inc=1, device_id={"gy": lax.rem(gy + d, ny)}, device_id_type=MESH)
    if direct:
        for flag, other in ((has_w, gx - 1), (has_e, gx + 1)):
            @pl.when(flag)
            def _(other=other):
                pl.semaphore_signal(barrier, inc=1, device_id={"gx": other}, device_id_type=MESH)
        greeted = ny - 1 + has_w.astype(jnp.int32) + has_e.astype(jnp.int32)
    else:
        for d in range(1, nx):
            pl.semaphore_signal(barrier, inc=1, device_id={"gx": lax.rem(gx + d, nx)}, device_id_type=MESH)
        greeted = nx + ny - 2

    loads = []
    for k, (src, dst) in enumerate([
        (perm_h, perm_v), (near_h, near_v), (far_h, far_v), (tr_h, tr_v),
        (acc_h, acc_v), (mob_h, mob_v), (res_h, res_v),
        (wc_h, wc_ref), (wr_h, wr_ref),
    ]):
        copy = pltpu.make_async_copy(src, dst, load_sem.at[k])
        copy.start()
        loads.append(copy)

    loads[0].wait()
    perm = perm_v.reshape(3 * cx * cy, nz)
    ps_u[...] = perm[pl.ds(cx * cy + cy - 1, cx, stride=cy), :]
    ps_l[...] = perm[pl.ds(cx * cy, cx, stride=cy), :]
    for k in (1, 2, 3):
        loads[k].wait()

    pl.semaphore_wait(barrier, greeted)

    def remote(src, dst, send, recv, target):
        return pltpu.make_async_remote_copy(
            src_ref=src, dst_ref=dst, send_sem=send, recv_sem=recv,
            device_id=target, device_id_type=MESH,
        )

    up, down = {"gy": gy + 1}, {"gy": gy - 1}
    east, west = {"gx": gx + 1}, {"gx": gx - 1}
    first_u = [
        remote(near_v, near_l, s0.at[0], r0.at[0], up),
        remote(ps_u, py_l, s0.at[1], r0.at[1], up),
    ]
    first_l = [
        remote(far_v, far_u, s0.at[2], r0.at[2], down),
        remote(tr_v, tr_u, s0.at[3], r0.at[3], down),
        remote(ps_l, py_u, s0.at[4], r0.at[4], down),
    ]
    first_e = [remote(perm_v.at[0, cx - 1], px_l, s0.at[5], r0.at[5], east)]
    first_w = [remote(perm_v.at[0, 0], px_u, s0.at[6], r0.at[6], west)]

    def start(to_u, to_l, to_e, to_w):
        for flag, copies in ((has_u, to_u), (has_l, to_l), (has_e, to_e), (has_w, to_w)):
            @pl.when(flag)
            def _(copies=copies):
                for copy in copies:
                    copy.start()

    def arrive(to_u, to_l, to_e, to_w):
        for flag, copies in ((has_u, to_l), (has_l, to_u), (has_e, to_w), (has_w, to_e)):
            @pl.when(flag)
            def _(copies=copies):
                for copy in copies:
                    copy.wait_recv()

    def sent(to_u, to_l, to_e, to_w):
        for flag, copies in ((has_u, to_u), (has_l, to_l), (has_e, to_e), (has_w, to_w)):
            @pl.when(flag)
            def _(copies=copies):
                for copy in copies:
                    copy.wait_send()

    start(first_u, first_l, first_e, first_w)

    def clear(flag, *refs):
        @pl.when(jnp.logical_not(flag))
        def _():
            for ref in refs:
                ref[...] = jnp.zeros(ref.shape, ref.dtype)

    clear(has_l, near_l, py_l, recv_l)
    clear(has_u, far_u, tr_u, py_u, recv_u)
    clear(has_w, px_l, recv_w)
    clear(has_e, px_u, recv_e)

    rows = 2 * cx
    row_iota = lax.broadcasted_iota(jnp.int32, (rows, cap), 0)
    layer_iota = lax.broadcasted_iota(jnp.int32, (nz, cap), 0)

    def slots(ref, base, onehot):
        index = ref[...]
        column = quotient(index, nz)
        layer = index - column * nz
        across = quotient(column, cy)
        along = column - across * cy - base
        onehot[...] = jnp.where(layer_iota == layer, 1.0, 0.0).astype(jnp.bfloat16)
        return row_iota == along * cx + across

    far_rows = slots(far_v, 0, z_far)
    near_rows = slots(near_v, cy - 2, z_near)

    def scatter(values, where_rows, onehot):
        parts = []
        for value in values:
            chosen = jnp.where(where_rows, value, 0.0)
            parts.extend(split_two(chosen))
        spread = lax.dot_general(
            jnp.concatenate(parts, axis=0), onehot[...], (((1,), (1,)), ((), ())),
            preferred_element_type=jnp.float32,
        )
        return [
            spread[2 * c * rows:(2 * c + 1) * rows] + spread[(2 * c + 1) * rows:(2 * c + 2) * rows]
            for c in range(len(values))
        ]

    def gather(block, where_rows, onehot):
        high, low = split_two(block)
        found = lax.dot_general(
            jnp.concatenate([high, low], axis=0), onehot[...], (((1,), (0,)), ((), ())),
            preferred_element_type=jnp.float32,
        )
        found = found[:3 * rows] + found[3 * rows:]
        return [
            jnp.sum(jnp.where(where_rows, found[c * rows:(c + 1) * rows], 0.0), axis=0, keepdims=True)
            for c in range(3)
        ]

    trans = tr_v[...]
    perm_x, perm_y, perm_z = perm_v[0], perm_v[1], perm_v[2]
    y_iota = lax.broadcasted_iota(jnp.int32, (cx, cy, nz), 1)
    z_iota = lax.broadcasted_iota(jnp.int32, (cx, cy, nz), 2)
    t_x = harmonic(perm_x[:-1], perm_x[1:])
    t_n = jnp.where(y_iota == cy - 1, 0.0, harmonic(perm_y, pltpu.roll(perm_y, cy - 1, 1)))
    t_s = jnp.where(y_iota == 0, 0.0, harmonic(perm_y, pltpu.roll(perm_y, 1, 1)))
    t_a = jnp.where(z_iota == nz - 1, 0.0, harmonic(perm_z, pltpu.roll(perm_z, nz - 1, 2)))
    t_b = jnp.where(z_iota == 0, 0.0, harmonic(perm_z, pltpu.roll(perm_z, 1, 2)))
    far_sum = scatter([trans], far_rows, z_far)[0]

    for k in range(4, 9):
        loads[k].wait()
    lin = (
        lax.broadcasted_iota(jnp.int32, (cx, cy, nz), 0) * (cy * nz) + y_iota * nz + z_iota
    )
    rhs0, rhs1, rhs2 = -res_v[0], -res_v[1], -res_v[2]
    for w in range(wells):
        rhs1 = rhs1 + jnp.where(lin == wc_ref[0, w], wr_ref[0, w], 0.0)
    arrive(first_u, first_l, first_e, first_w)
    trans_u = tr_u[...]
    near_sum = scatter([trans_u], near_rows, z_near)[0]
    t_w0 = harmonic(perm_x[0], px_l[...])
    t_e1 = harmonic(perm_x[cx - 1], px_u[...])
    t_e = jnp.concatenate([t_x, t_e1[None]], axis=0)
    t_w = jnp.concatenate([t_w0[None], t_x], axis=0)
    t_s0 = harmonic(ps_l[...], py_l[...])
    t_n1 = harmonic(ps_u[...], py_u[...])

    flat = cx * cy
    tot[...] = (t_e + t_w + t_n + t_s + t_a + t_b).reshape(flat, nz)

    def add_rows(ref, start_row, value):
        place = (pl.ds(start_row, cx, stride=cy), slice(None))
        ref[place] = ref[place] + value

    add_rows(tot, 0, far_sum[:cx] + t_s0)
    add_rows(tot, 1, far_sum[cx:])
    add_rows(tot, cy - 2, near_sum[:cx])
    add_rows(tot, cy - 1, near_sum[cx:] + t_n1)

    total = tot[...].reshape(cx, cy, nz)
    mob = [[mob_v[a, b] for b in range(3)] for a in range(3)]
    diag = [[acc_v[a, b] + total * mob[a][b] for b in range(3)] for a in range(3)]
    w1 = diag[0][1] / diag[1][1]
    w2 = diag[0][2] / diag[2][2]
    w_v[0] = w1
    w_v[1] = w2
    blk = [[diag[0][b] - w1 * diag[1][b] - w2 * diag[2][b] for b in range(3)], diag[1], diag[2]]

    def part(a, b, c, d):
        return blk[a][b] * blk[c][d] - blk[a][d] * blk[c][b]

    cof = [
        [part(1, 1, 2, 2), -part(1, 0, 2, 2), part(1, 0, 2, 1)],
        [-part(0, 1, 2, 2), part(0, 0, 2, 2), -part(0, 0, 2, 1)],
        [part(0, 1, 1, 2), -part(0, 0, 1, 2), part(0, 0, 1, 1)],
    ]
    det = blk[0][0] * cof[0][0] + blk[0][1] * cof[0][1] + blk[0][2] * cof[0][2]
    inverse_det = 1.0 / det
    pre = [[cof[b][a] * inverse_det for b in range(3)] for a in range(3)]
    for a in range(3):
        for b in range(3):
            inv[a, b] = pre[a][b]
            mix[a, b] = mob[a][0] * pre[0][b] + mob[a][1] * pre[1][b] + mob[a][2] * pre[2][b]

    ys[0, 0] = rhs0 - w1 * rhs1 - w2 * rhs2
    ys[0, 1] = rhs1
    ys[0, 2] = rhs2

    def product(left, right):
        return jnp.sum(jnp.sum(ys[left] * ys[right], axis=(0, 1)), axis=0, keepdims=True)

    pending = [(first_u, first_l, first_e, first_w)]
    for it in range(KRYLOV):
        y = [ys[it, c] for c in range(3)]
        field = []
        for a in range(3):
            value = mix[a, 0] * y[0] + mix[a, 1] * y[1] + mix[a, 2] * y[2]
            field.append(value)
            flux[pl.ds(a * flat, flat), :] = value.reshape(flat, nz)
            send_e[it, a] = value[cx - 1]
            send_w[it, a] = value[0]
        for a in range(3):
            for r in range(2):
                at = pl.ds((2 * a + r) * cx, cx)
                send_u[it, at, :] = flux[pl.ds(a * flat + cy - 2 + r, cx, stride=cy), :]
                send_l[it, at, :] = flux[pl.ds(a * flat + r, cx, stride=cy), :]
        copies = (
            [remote(send_u.at[it], recv_l.at[it], s1.at[it, 0], r1.at[it, 0], up)],
            [remote(send_l.at[it], recv_u.at[it], s1.at[it, 1], r1.at[it, 1], down)],
            [remote(send_e.at[it], recv_w.at[it], s1.at[it, 2], r1.at[it, 2], east)],
            [remote(send_w.at[it], recv_e.at[it], s1.at[it, 3], r1.at[it, 3], west)],
        )
        start(*copies)
        pending.append(copies)
        if it == 0:
            near_rows_l = slots(near_l, cy - 2, z_near_l)
            far_rows_u = slots(far_u, 0, z_far_u)
        inner = []
        for a in range(3):
            f = field[a]
            near_sums = (
                t_n * pltpu.roll(f, cy - 1, 1) + t_s * pltpu.roll(f, 1, 1)
                + t_a * pltpu.roll(f, nz - 1, 2) + t_b * pltpu.roll(f, 1, 2)
            )
            inner.append(near_sums)
        if it == KRYLOV - 1:
            rows_early = [product(left, right) for left, right in PAIRS if right < KRYLOV]
        arrive(*copies)
        below, above = recv_l[it], recv_u[it]
        got_l = gather(below, near_rows_l, z_near_l)
        got_u = gather(above, far_rows_u, z_far_u)
        fault_l = scatter([trans * g for g in got_l], far_rows, z_far)
        fault_u = scatter([trans_u * g for g in got_u], near_rows, z_near)
        for a in range(3):
            f = field[a]
            value = (
                inner[a]
                + t_e * jnp.concatenate([f[1:], recv_e[it, a][None]], axis=0)
                + t_w * jnp.concatenate([recv_w[it, a][None], f[:-1]], axis=0)
            )
            offs[pl.ds(a * flat, flat), :] = value.reshape(flat, nz)
            halo_s = below[(2 * a + 1) * cx:(2 * a + 2) * cx]
            halo_n = above[2 * a * cx:(2 * a + 1) * cx]
            add_rows(offs, a * flat, fault_l[a][:cx] + t_s0 * halo_s)
            add_rows(offs, a * flat + 1, fault_l[a][cx:])
            add_rows(offs, a * flat + cy - 2, fault_u[a][:cx])
            add_rows(offs, a * flat + cy - 1, fault_u[a][cx:] + t_n1 * halo_n)
        o = [offs[pl.ds(a * flat, flat), :].reshape(cx, cy, nz) for a in range(3)]
        ys[it + 1, 0] = o[0] - w_v[0] * o[1] - w_v[1] * o[2]
        ys[it + 1, 1] = o[1]
        ys[it + 1, 2] = o[2]

    rows_late = [product(left, KRYLOV) for left in range(KRYLOV + 1)]
    count = -(-len(PAIRS) // 8) * 8
    blank = jnp.zeros((count - len(PAIRS), nz), jnp.float32)
    table = jnp.concatenate(rows_early + rows_late + [blank], axis=0)
    on_lane = (
        lax.broadcasted_iota(jnp.int32, (count, nz), 0)
        == lax.broadcasted_iota(jnp.int32, (count, nz), 1)
    )

    def to_lanes(block):
        filled = jnp.broadcast_to(jnp.sum(block, axis=1, keepdims=True), block.shape)
        return jnp.sum(jnp.where(on_lane, filled, 0.0), axis=0, keepdims=True)

    def total_of(ref, size):
        value = ref[0]
        for d in range(1, size):
            value = value + ref[d]
        return value

    line = to_lanes(table)
    shared = []
    if direct:
        me = gx * ny + gy
        red_y[me] = line
        for dx in range(nx):
            for dy in range(ny):
                if dx or dy:
                    k = dx * ny + dy
                    target = {"gx": lax.rem(gx + dx, nx), "gy": lax.rem(gy + dy, ny)}
                    shared.append(remote(red_y.at[me], red_y.at[me], sy.at[k], ry.at[k], target))
        for copy in shared:
            copy.start()
        for copy in shared:
            copy.wait_recv()
        line = total_of(red_y, nx * ny)
    else:
        for axis, me, size, ref, send, recv in (
            ("gy", gy, ny, red_y, sy, ry), ("gx", gx, nx, red_x, sx, rx),
        ):
            ref[me] = line
            stage = [
                remote(ref.at[me], ref.at[me], send.at[d], recv.at[d], {axis: lax.rem(me + d, size)})
                for d in range(1, size)
            ]
            for copy in stage:
                copy.start()
            for copy in stage:
                copy.wait_recv()
            shared.extend(stage)
            line = total_of(ref, size)
    spread = jnp.where(on_lane, jnp.broadcast_to(line, (count, nz)), 0.0)
    sums = jnp.broadcast_to(jnp.sum(spread, axis=1, keepdims=True), (count, nz))

    def entry(left, right):
        k = PAIRS.index((min(left, right), max(left, right)))
        return sums[k:k + 1]

    normal = [
        [(entry(a, b) - entry(a, b + 1)) - (entry(a + 1, b) - entry(a + 1, b + 1)) for b in range(KRYLOV)]
        for a in range(KRYLOV)
    ]
    coefs = solve_small(normal, [entry(0, a) - entry(0, a + 1) for a in range(KRYLOV)])
    left_over = [1.0 - coefs[0]] + [coefs[k] - coefs[k + 1] for k in range(KRYLOV - 1)] + [coefs[-1]]
    coefs = [c.reshape(1, 1, nz) for c in coefs]
    left_over = [c.reshape(1, 1, nz) for c in left_over]
    mixed = []
    for c in range(3):
        combined = coefs[0] * ys[0, c]
        rest = left_over[0] * ys[0, c]
        for k in range(1, KRYLOV):
            combined = combined + coefs[k] * ys[k, c]
            rest = rest + left_over[k] * ys[k, c]
        mixed.append(combined)
        out_o[c] = rest + left_over[KRYLOV] * ys[KRYLOV, c]
    for c in range(3):
        upd_o[c] = inv[c, 0] * mixed[0] + inv[c, 1] * mixed[1] + inv[c, 2] * mixed[2]
    for group in pending:
        sent(*group)
    for copy in shared:
        copy.wait_send()


def solution(mesh):
    nx, ny = mesh.shape["gx"], mesh.shape["gy"]
    placed = (
        P(None, "gx", "gy", None),
        P(None, None, "gx", "gy", None),
        P(None, None, "gx", "gy", None),
        P(None, "gx", "gy", None),
    ) + (P("gx", "gy", None),) * 5

    def shards(residual_in, accumulation, mobility, permeability, fault_near, fault_far, fault_trans, well_cells, well_rates):
        _, cx, cy, nz = residual_in.shape
        cap = fault_near.shape[-1]
        wells = well_cells.shape[-1]
        flat = cx * cy
        direct = nx <= KRYLOV + 2 and nx * ny <= 64
        stages = (nx * ny if direct else ny, nx)
        f32, i32, bf16 = jnp.float32, jnp.int32, jnp.bfloat16
        vm = pltpu.VMEM
        dma = pltpu.SemaphoreType.DMA
        scratch = [
            vm((3, cx, cy, nz), f32), vm((3, 3, cx, cy, nz), f32), vm((3, 3, cx, cy, nz), f32),
            vm((3, cx, cy, nz), f32),
            vm((1, cap), i32), vm((1, cap), i32), vm((1, cap), f32),
            pltpu.SMEM((1, wells), i32), pltpu.SMEM((1, wells), f32),
            vm((1, cap), i32), vm((1, cap), f32), vm((1, cap), i32),
        ]
        scratch += [vm((cx, nz), f32)] * 4 + [vm((cy, nz), f32)] * 2
        scratch += [
            vm((flat, nz), f32), vm((3, 3, cx, cy, nz), f32), vm((3, 3, cx, cy, nz), f32),
            vm((2, cx, cy, nz), f32), vm((KRYLOV + 1, 3, cx, cy, nz), f32),
            vm((3 * flat, nz), f32), vm((3 * flat, nz), f32),
        ]
        scratch += [vm((KRYLOV, 6 * cx, nz), f32)] * 2 + [vm((KRYLOV, 3, cy, nz), f32)] * 2
        scratch += [vm((KRYLOV, 6 * cx, nz), f32)] * 2 + [vm((KRYLOV, 3, cy, nz), f32)] * 2
        scratch += [vm((nz, cap), bf16)] * 4
        scratch += [vm((stages[0], 1, nz), f32), vm((stages[1], 1, nz), f32)]
        scratch += [
            dma((9,)), dma((7,)), dma((7,)), dma((KRYLOV, 4)), dma((KRYLOV, 4)),
            dma((stages[0],)), dma((stages[0],)), dma((stages[1],)), dma((stages[1],)),
        ]
        anywhere = pl.BlockSpec(memory_space=pl.ANY)
        inside = pl.BlockSpec(memory_space=pltpu.VMEM)
        shape = jax.ShapeDtypeStruct(residual_in.shape, f32)
        return pl.pallas_call(
            functools.partial(kernel, nx, ny, cx, cy, nz, cap, wells, direct),
            out_shape=(shape, shape),
            in_specs=[anywhere] * 9,
            out_specs=(inside, inside),
            scratch_shapes=scratch,
            compiler_params=pltpu.CompilerParams(collective_id=0, has_side_effects=True),
            name="newton",
        )(
            residual_in, accumulation, mobility, permeability,
            fault_near.reshape(1, cap), fault_far.reshape(1, cap), fault_trans.reshape(1, cap),
            well_cells.reshape(1, wells), well_rates.reshape(1, wells),
        )

    out = P(None, "gx", "gy", None)
    return jax.shard_map(shards, mesh=mesh, in_specs=placed, out_specs=(out, out), check_vma=False)
```

```python
import functools

import jax
import jax.numpy as jnp
from jax import lax
from jax.experimental import pallas as pl
from jax.experimental.pallas import tpu as pltpu
from jax.sharding import PartitionSpec as P

KRYLOV = 3
PAIRS = [(a, b) for b in range(KRYLOV + 1) for a in range(b + 1)]
MESH = pl.DeviceIdType.MESH


def harmonic(a, b):
    return 2.0 * a * b / (a + b)


def quotient(value, by):
    if by & (by - 1) == 0:
        return lax.shift_right_logical(value, jnp.int32(by.bit_length() - 1))
    return value // by


def split_two(value):
    high = value.astype(jnp.bfloat16)
    low = (value - high.astype(jnp.float32)).astype(jnp.bfloat16)
    return high, low


def solve_small(matrix, rhs_values):
    size = len(rhs_values)
    rows = [list(line) for line in matrix]
    values = list(rhs_values)
    for column in range(size):
        for lower in range(column + 1, size):
            factor = rows[lower][column] / rows[column][column]
            rows[lower] = [e - factor * p for e, p in zip(rows[lower], rows[column])]
            values[lower] = values[lower] - factor * values[column]
    solved = [0.0] * size
    for column in reversed(range(size)):
        partial = values[column]
        for later in range(column + 1, size):
            partial = partial - rows[column][later] * solved[later]
        solved[column] = partial / rows[column][column]
    return solved


def kernel(
    nx, ny, cx, cy, nz, cap, wells, direct,
    res_h, acc_h, mob_h, perm_h, near_h, far_h, tr_h, wc_h, wr_h,
    upd_o, out_o,
    res_v, acc_v, mob_v, perm_v, near_v, far_v, tr_v,
    wc_ref, wr_ref,
    far_u, tr_u, near_l,
    ps_u, ps_l, py_l, py_u, px_l, px_u,
    tot, inv, mix, w_v, ys, flux, offs,
    send_u, send_l, send_e, send_w, recv_l, recv_u, recv_w, recv_e,
    z_far, z_near, z_near_l, z_far_u,
    m_far, m_near, m_near_l, m_far_u,
    red_y, red_x,
    load_sem, s0, r0, s1, r1, sy, ry, sx, rx,
):
    gx, gy = lax.axis_index("gx"), lax.axis_index("gy")
    has_l, has_u = gy > 0, gy < ny - 1
    has_w, has_e = gx > 0, gx < nx - 1

    loads = []
    for k, (src, dst) in enumerate([
        (perm_h, perm_v), (near_h, near_v), (far_h, far_v), (tr_h, tr_v),
        (acc_h, acc_v), (mob_h, mob_v), (res_h, res_v),
        (wc_h, wc_ref), (wr_h, wr_ref),
    ]):
        copy = pltpu.make_async_copy(src, dst, load_sem.at[k])
        copy.start()
        loads.append(copy)

    barrier = pltpu.get_barrier_semaphore()
    for d in range(1, ny):
        pl.semaphore_signal(barrier, inc=1, device_id={"gy": lax.rem(gy + d, ny)}, device_id_type=MESH)
    if direct:
        for flag, other in ((has_w, gx - 1), (has_e, gx + 1)):
            @pl.when(flag)
            def _(other=other):
                pl.semaphore_signal(barrier, inc=1, device_id={"gx": other}, device_id_type=MESH)
        greeted = ny - 1 + has_w.astype(jnp.int32) + has_e.astype(jnp.int32)
    else:
        for d in range(1, nx):
            pl.semaphore_signal(barrier, inc=1, device_id={"gx": lax.rem(gx + d, nx)}, device_id_type=MESH)
        greeted = nx + ny - 2

    loads[0].wait()
    perm = perm_v.reshape(3 * cx * cy, nz)
    ps_u[...] = perm[pl.ds(cx * cy + cy - 1, cx, stride=cy), :]
    ps_l[...] = perm[pl.ds(cx * cy, cx, stride=cy), :]
    for k in (1, 2, 3):
        loads[k].wait()

    pl.semaphore_wait(barrier, greeted)

    def remote(src, dst, send, recv, target):
        return pltpu.make_async_remote_copy(
            src_ref=src, dst_ref=dst, send_sem=send, recv_sem=recv,
            device_id=target, device_id_type=MESH,
        )

    up, down = {"gy": gy + 1}, {"gy": gy - 1}
    east, west = {"gx": gx + 1}, {"gx": gx - 1}
    first_u = [
        remote(near_v, near_l, s0.at[0], r0.at[0], up),
        remote(ps_u, py_l, s0.at[1], r0.at[1], up),
    ]
    first_l = [
        remote(far_v, far_u, s0.at[2], r0.at[2], down),
        remote(tr_v, tr_u, s0.at[3], r0.at[3], down),
        remote(ps_l, py_u, s0.at[4], r0.at[4], down),
    ]
    first_e = [remote(perm_v.at[0, cx - 1], px_l, s0.at[5], r0.at[5], east)]
    first_w = [remote(perm_v.at[0, 0], px_u, s0.at[6], r0.at[6], west)]

    def start(to_u, to_l, to_e, to_w):
        for flag, copies in ((has_u, to_u), (has_l, to_l), (has_e, to_e), (has_w, to_w)):
            @pl.when(flag)
            def _(copies=copies):
                for copy in copies:
                    copy.start()

    def arrive(to_u, to_l, to_e, to_w):
        for flag, copies in ((has_u, to_l), (has_l, to_u), (has_e, to_w), (has_w, to_e)):
            @pl.when(flag)
            def _(copies=copies):
                for copy in copies:
                    copy.wait_recv()

    def sent(to_u, to_l, to_e, to_w):
        for flag, copies in ((has_u, to_u), (has_l, to_l), (has_e, to_e), (has_w, to_w)):
            @pl.when(flag)
            def _(copies=copies):
                for copy in copies:
                    copy.wait_send()

    start(first_u, first_l, first_e, first_w)

    def clear(flag, *refs):
        @pl.when(jnp.logical_not(flag))
        def _():
            for ref in refs:
                ref[...] = jnp.zeros(ref.shape, ref.dtype)

    clear(has_l, near_l, py_l, recv_l)
    clear(has_u, far_u, tr_u, py_u, recv_u)
    clear(has_w, px_l, recv_w)
    clear(has_e, px_u, recv_e)

    rows = 2 * cx
    row_iota = lax.broadcasted_iota(jnp.int32, (rows, cap), 0)
    layer_iota = lax.broadcasted_iota(jnp.int32, (nz, cap), 0)

    def slots(ref, base, onehot, mask):
        index = ref[...]
        column = quotient(index, nz)
        layer = index - column * nz
        across = quotient(column, cy)
        along = column - across * cy - base
        hot = jnp.where(layer_iota == layer, 1.0, 0.0).astype(jnp.bfloat16)
        for copy in range(onehot.shape[0] // nz):
            onehot[pl.ds(copy * nz, nz), :] = hot
        mask[...] = jnp.where(row_iota == along * cx + across, 1.0, 0.0).astype(mask.dtype)

    slots(far_v, 0, z_far, m_far)
    slots(near_v, cy - 2, z_near, m_near)

    def scatter(values, mask, onehot):
        parts = []
        for value in values:
            parts.extend(mask[...] * half for half in split_two(value))
        spread = lax.dot_general(
            jnp.concatenate(parts, axis=0), onehot[...], (((1,), (1,)), ((), ())),
            preferred_element_type=jnp.float32,
        )
        return [
            spread[2 * c * rows:(2 * c + 1) * rows] + spread[(2 * c + 1) * rows:(2 * c + 2) * rows]
            for c in range(len(values))
        ]

    def gather(block, mask, onehot):
        found = lax.dot_general(
            jnp.concatenate(split_two(block), axis=1), onehot[...], (((1,), (0,)), ((), ())),
            preferred_element_type=jnp.float32,
        )
        return [
            jnp.sum(mask[...] * found[c * rows:(c + 1) * rows], axis=0, keepdims=True)
            for c in range(3)
        ]

    trans = tr_v[...]
    perm_x, perm_y, perm_z = perm_v[0], perm_v[1], perm_v[2]
    y_iota = lax.broadcasted_iota(jnp.int32, (cx, cy, nz), 1)
    z_iota = lax.broadcasted_iota(jnp.int32, (cx, cy, nz), 2)
    t_x = harmonic(perm_x[:-1], perm_x[1:])
    t_n = jnp.where(y_iota == cy - 1, 0.0, harmonic(perm_y, pltpu.roll(perm_y, cy - 1, 1)))
    t_s = jnp.where(y_iota == 0, 0.0, harmonic(perm_y, pltpu.roll(perm_y, 1, 1)))
    t_a = jnp.where(z_iota == nz - 1, 0.0, harmonic(perm_z, pltpu.roll(perm_z, nz - 1, 2)))
    t_b = jnp.where(z_iota == 0, 0.0, harmonic(perm_z, pltpu.roll(perm_z, 1, 2)))
    far_sum = scatter([trans], m_far, z_far)[0]

    for k in range(4, 9):
        loads[k].wait()
    lin = (
        lax.broadcasted_iota(jnp.int32, (cx, cy, nz), 0) * (cy * nz) + y_iota * nz + z_iota
    )
    rhs0, rhs1, rhs2 = -res_v[0], -res_v[1], -res_v[2]
    for w in range(wells):
        rhs1 = rhs1 + jnp.where(lin == wc_ref[0, w], wr_ref[0, w], 0.0)
    arrive(first_u, first_l, first_e, first_w)
    trans_u = tr_u[...]
    near_sum = scatter([trans_u], m_near, z_near)[0]
    t_w0 = harmonic(perm_x[0], px_l[...])
    t_e1 = harmonic(perm_x[cx - 1], px_u[...])
    t_e = jnp.concatenate([t_x, t_e1[None]], axis=0)
    t_w = jnp.concatenate([t_w0[None], t_x], axis=0)
    t_s0 = harmonic(ps_l[...], py_l[...])
    t_n1 = harmonic(ps_u[...], py_u[...])

    flat = cx * cy
    tot[...] = (t_e + t_w + t_n + t_s + t_a + t_b).reshape(flat, nz)

    def add_rows(ref, start_row, value):
        place = (pl.ds(start_row, cx, stride=cy), slice(None))
        ref[place] = ref[place] + value

    add_rows(tot, 0, far_sum[:cx] + t_s0)
    add_rows(tot, 1, far_sum[cx:])
    add_rows(tot, cy - 2, near_sum[:cx])
    add_rows(tot, cy - 1, near_sum[cx:] + t_n1)

    total = tot[...].reshape(cx, cy, nz)
    mob = [[mob_v[a, b] for b in range(3)] for a in range(3)]
    diag = [[acc_v[a, b] + total * mob[a][b] for b in range(3)] for a in range(3)]
    w1 = diag[0][1] / diag[1][1]
    w2 = diag[0][2] / diag[2][2]
    w_v[0] = w1
    w_v[1] = w2
    blk = [[diag[0][b] - w1 * diag[1][b] - w2 * diag[2][b] for b in range(3)], diag[1], diag[2]]

    def part(a, b, c, d):
        return blk[a][b] * blk[c][d] - blk[a][d] * blk[c][b]

    cof = [
        [part(1, 1, 2, 2), -part(1, 0, 2, 2), part(1, 0, 2, 1)],
        [-part(0, 1, 2, 2), part(0, 0, 2, 2), -part(0, 0, 2, 1)],
        [part(0, 1, 1, 2), -part(0, 0, 1, 2), part(0, 0, 1, 1)],
    ]
    det = blk[0][0] * cof[0][0] + blk[0][1] * cof[0][1] + blk[0][2] * cof[0][2]
    inverse_det = 1.0 / det
    pre = [[cof[b][a] * inverse_det for b in range(3)] for a in range(3)]
    for a in range(3):
        for b in range(3):
            inv[a, b] = pre[a][b]
            mix[a, b] = mob[a][0] * pre[0][b] + mob[a][1] * pre[1][b] + mob[a][2] * pre[2][b]

    ys[0, 0] = rhs0 - w1 * rhs1 - w2 * rhs2
    ys[0, 1] = rhs1
    ys[0, 2] = rhs2

    def product(left, right):
        return jnp.sum(jnp.sum(ys[left] * ys[right], axis=(0, 1)), axis=0, keepdims=True)

    pending = [(first_u, first_l, first_e, first_w)]
    for it in range(KRYLOV):
        y = [ys[it, c] for c in range(3)]
        field = []
        for a in range(3):
            value = mix[a, 0] * y[0] + mix[a, 1] * y[1] + mix[a, 2] * y[2]
            field.append(value)
            flux[pl.ds(a * flat, flat), :] = value.reshape(flat, nz)
            send_e[it, a] = value[cx - 1]
            send_w[it, a] = value[0]
        for a in range(3):
            for r in range(2):
                at = pl.ds((2 * a + r) * cx, cx)
                send_u[it, at, :] = flux[pl.ds(a * flat + cy - 2 + r, cx, stride=cy), :]
                send_l[it, at, :] = flux[pl.ds(a * flat + r, cx, stride=cy), :]
        copies = (
            [remote(send_u.at[it], recv_l.at[it], s1.at[it, 0], r1.at[it, 0], up)],
            [remote(send_l.at[it], recv_u.at[it], s1.at[it, 1], r1.at[it, 1], down)],
            [remote(send_e.at[it], recv_w.at[it], s1.at[it, 2], r1.at[it, 2], east)],
            [remote(send_w.at[it], recv_e.at[it], s1.at[it, 3], r1.at[it, 3], west)],
        )
        start(*copies)
        pending.append(copies)
        if it == 0:
            slots(near_l, cy - 2, z_near_l, m_near_l)
            slots(far_u, 0, z_far_u, m_far_u)
        inner = []
        for a in range(3):
            f = field[a]
            near_sums = (
                t_n * pltpu.roll(f, cy - 1, 1) + t_s * pltpu.roll(f, 1, 1)
                + t_a * pltpu.roll(f, nz - 1, 2) + t_b * pltpu.roll(f, 1, 2)
            )
            inner.append(near_sums)
        if it == KRYLOV - 1:
            rows_early = [product(left, right) for left, right in PAIRS if right < KRYLOV]
        arrive(*copies)
        below, above = recv_l[it], recv_u[it]
        got_l = gather(below, m_near_l, z_near_l)
        got_u = gather(above, m_far_u, z_far_u)
        fault_l = scatter([trans * g for g in got_l], m_far, z_far)
        fault_u = scatter([trans_u * g for g in got_u], m_near, z_near)
        for a in range(3):
            f = field[a]
            value = (
                inner[a]
                + t_e * jnp.concatenate([f[1:], recv_e[it, a][None]], axis=0)
                + t_w * jnp.concatenate([recv_w[it, a][None], f[:-1]], axis=0)
            )
            offs[pl.ds(a * flat, flat), :] = value.reshape(flat, nz)
            halo_s = below[(2 * a + 1) * cx:(2 * a + 2) * cx]
            halo_n = above[2 * a * cx:(2 * a + 1) * cx]
            add_rows(offs, a * flat, fault_l[a][:cx] + t_s0 * halo_s)
            add_rows(offs, a * flat + 1, fault_l[a][cx:])
            add_rows(offs, a * flat + cy - 2, fault_u[a][:cx])
            add_rows(offs, a * flat + cy - 1, fault_u[a][cx:] + t_n1 * halo_n)
        o = [offs[pl.ds(a * flat, flat), :].reshape(cx, cy, nz) for a in range(3)]
        ys[it + 1, 0] = o[0] - w_v[0] * o[1] - w_v[1] * o[2]
        ys[it + 1, 1] = o[1]
        ys[it + 1, 2] = o[2]

    rows_late = [product(left, KRYLOV) for left in range(KRYLOV + 1)]
    count = -(-len(PAIRS) // 8) * 8
    blank = jnp.zeros((count - len(PAIRS), nz), jnp.float32)
    table = jnp.concatenate(rows_early + rows_late + [blank], axis=0)
    on_lane = (
        lax.broadcasted_iota(jnp.int32, (count, nz), 0)
        == lax.broadcasted_iota(jnp.int32, (count, nz), 1)
    )

    def to_lanes(block):
        filled = jnp.broadcast_to(jnp.sum(block, axis=1, keepdims=True), block.shape)
        return jnp.sum(jnp.where(on_lane, filled, 0.0), axis=0, keepdims=True)

    def total_of(ref, size):
        value = ref[0]
        for d in range(1, size):
            value = value + ref[d]
        return value

    line = to_lanes(table)
    shared = []
    if direct:
        me = gx * ny + gy
        red_y[me] = line
        for dx in range(nx):
            for dy in range(ny):
                if dx or dy:
                    k = dx * ny + dy
                    target = {"gx": lax.rem(gx + dx, nx), "gy": lax.rem(gy + dy, ny)}
                    shared.append(remote(red_y.at[me], red_y.at[me], sy.at[k], ry.at[k], target))
        for copy in shared:
            copy.start()
        for copy in shared:
            copy.wait_recv()
        line = total_of(red_y, nx * ny)
    else:
        for axis, me, size, ref, send, recv in (
            ("gy", gy, ny, red_y, sy, ry), ("gx", gx, nx, red_x, sx, rx),
        ):
            ref[me] = line
            stage = [
                remote(ref.at[me], ref.at[me], send.at[d], recv.at[d], {axis: lax.rem(me + d, size)})
                for d in range(1, size)
            ]
            for copy in stage:
                copy.start()
            for copy in stage:
                copy.wait_recv()
            shared.extend(stage)
            line = total_of(ref, size)
    spread = jnp.where(on_lane, jnp.broadcast_to(line, (count, nz)), 0.0)
    sums = jnp.broadcast_to(jnp.sum(spread, axis=1, keepdims=True), (count, nz))

    def entry(left, right):
        k = PAIRS.index((min(left, right), max(left, right)))
        return sums[k:k + 1]

    normal = [
        [(entry(a, b) - entry(a, b + 1)) - (entry(a + 1, b) - entry(a + 1, b + 1)) for b in range(KRYLOV)]
        for a in range(KRYLOV)
    ]
    coefs = solve_small(normal, [entry(0, a) - entry(0, a + 1) for a in range(KRYLOV)])
    left_over = [1.0 - coefs[0]] + [coefs[k] - coefs[k + 1] for k in range(KRYLOV - 1)] + [coefs[-1]]
    coefs = [c.reshape(1, 1, nz) for c in coefs]
    left_over = [c.reshape(1, 1, nz) for c in left_over]
    mixed = []
    for c in range(3):
        combined = coefs[0] * ys[0, c]
        rest = left_over[0] * ys[0, c]
        for k in range(1, KRYLOV):
            combined = combined + coefs[k] * ys[k, c]
            rest = rest + left_over[k] * ys[k, c]
        mixed.append(combined)
        out_o[c] = rest + left_over[KRYLOV] * ys[KRYLOV, c]
    for c in range(3):
        upd_o[c] = inv[c, 0] * mixed[0] + inv[c, 1] * mixed[1] + inv[c, 2] * mixed[2]
    for group in pending:
        sent(*group)
    for copy in shared:
        copy.wait_send()


def put_out(update_v, rest_v, update_h, rest_h, sem):
    copies = [
        pltpu.make_async_copy(update_v, update_h, sem.at[0]),
        pltpu.make_async_copy(rest_v, rest_h, sem.at[1]),
    ]
    for copy in copies:
        copy.start()
    for copy in copies:
        copy.wait()


def solution(mesh):
    nx, ny = mesh.shape["gx"], mesh.shape["gy"]
    placed = (
        P(None, "gx", "gy", None),
        P(None, None, "gx", "gy", None),
        P(None, None, "gx", "gy", None),
        P(None, "gx", "gy", None),
    ) + (P("gx", "gy", None),) * 5

    def shards(residual_in, accumulation, mobility, permeability, fault_near, fault_far, fault_trans, well_cells, well_rates):
        _, cx, cy, nz = residual_in.shape
        cap = fault_near.shape[-1]
        wells = well_cells.shape[-1]
        flat = cx * cy
        direct = nx <= KRYLOV + 2 and nx * ny <= 64
        stages = (nx * ny if direct else ny, nx)
        f32, i32, bf16 = jnp.float32, jnp.int32, jnp.bfloat16
        vm = pltpu.VMEM
        dma = pltpu.SemaphoreType.DMA
        scratch = [
            vm((3, cx, cy, nz), f32), vm((3, 3, cx, cy, nz), f32), vm((3, 3, cx, cy, nz), f32),
            vm((3, cx, cy, nz), f32),
            vm((1, cap), i32), vm((1, cap), i32), vm((1, cap), f32),
            pltpu.SMEM((1, wells), i32), pltpu.SMEM((1, wells), f32),
            vm((1, cap), i32), vm((1, cap), f32), vm((1, cap), i32),
        ]
        scratch += [vm((cx, nz), f32)] * 4 + [vm((cy, nz), f32)] * 2
        scratch += [
            vm((flat, nz), f32), vm((3, 3, cx, cy, nz), f32), vm((3, 3, cx, cy, nz), f32),
            vm((2, cx, cy, nz), f32), vm((KRYLOV + 1, 3, cx, cy, nz), f32),
            vm((3 * flat, nz), f32), vm((3 * flat, nz), f32),
        ]
        scratch += [vm((KRYLOV, 6 * cx, nz), f32)] * 2 + [vm((KRYLOV, 3, cy, nz), f32)] * 2
        scratch += [vm((KRYLOV, 6 * cx, nz), f32)] * 2 + [vm((KRYLOV, 3, cy, nz), f32)] * 2
        scratch += [vm((nz, cap), bf16)] * 2 + [vm((2 * nz, cap), bf16)] * 2
        scratch += [vm((2 * cx, cap), bf16)] * 2 + [vm((2 * cx, cap), f32)] * 2
        scratch += [vm((stages[0], 1, nz), f32), vm((stages[1], 1, nz), f32)]
        scratch += [
            dma((9,)), dma((7,)), dma((7,)), dma((KRYLOV, 4)), dma((KRYLOV, 4)),
            dma((stages[0],)), dma((stages[0],)), dma((stages[1],)), dma((stages[1],)),
        ]
        anywhere = pl.BlockSpec(memory_space=pl.ANY)
        inside = pl.BlockSpec(memory_space=pltpu.VMEM)
        held = pltpu.VMEM(residual_in.shape, f32)
        shape = jax.ShapeDtypeStruct(residual_in.shape, f32)
        update, rest = pl.pallas_call(
            functools.partial(kernel, nx, ny, cx, cy, nz, cap, wells, direct),
            out_shape=(held, held),
            in_specs=[anywhere] * 9,
            out_specs=(inside, inside),
            scratch_shapes=scratch,
            compiler_params=pltpu.CompilerParams(collective_id=0, has_side_effects=True),
            name="newton",
        )(
            residual_in, accumulation, mobility, permeability,
            fault_near.reshape(1, cap), fault_far.reshape(1, cap), fault_trans.reshape(1, cap),
            well_cells.reshape(1, wells), well_rates.reshape(1, wells),
        )
        return pl.pallas_call(
            put_out,
            out_shape=(shape, shape),
            in_specs=[anywhere] * 2,
            out_specs=(anywhere, anywhere),
            scratch_shapes=[dma((2,))],
            compiler_params=pltpu.CompilerParams(vmem_limit_bytes=1 << 20),
            name="put_out",
        )(*(pltpu.with_memory_space_constraint(v, pltpu.MemorySpace.VMEM) for v in (update, rest)))

    out = P(None, "gx", "gy", None)
    return jax.shard_map(shards, mesh=mesh, in_specs=placed, out_specs=(out, out), check_vma=False)
```

```python
import functools

import jax
import jax.numpy as jnp
from jax import lax
from jax.experimental import pallas as pl
from jax.experimental.pallas import tpu as pltpu
from jax.sharding import PartitionSpec as P

KRYLOV = 3
PAIRS = [(a, b) for b in range(KRYLOV + 1) for a in range(b + 1)]
MESH = pl.DeviceIdType.MESH


def harmonic(a, b):
    return 2.0 * a * b / (a + b)


def quotient(value, by):
    if by & (by - 1) == 0:
        return lax.shift_right_logical(value, jnp.int32(by.bit_length() - 1))
    return value // by


def split_two(value):
    high = value.astype(jnp.bfloat16)
    low = (value - high.astype(jnp.float32)).astype(jnp.bfloat16)
    return high, low


def solve_small(matrix, rhs_values):
    size = len(rhs_values)
    rows = [list(line) for line in matrix]
    values = list(rhs_values)
    for column in range(size):
        for lower in range(column + 1, size):
            factor = rows[lower][column] / rows[column][column]
            rows[lower] = [e - factor * p for e, p in zip(rows[lower], rows[column])]
            values[lower] = values[lower] - factor * values[column]
    solved = [0.0] * size
    for column in reversed(range(size)):
        partial = values[column]
        for later in range(column + 1, size):
            partial = partial - rows[column][later] * solved[later]
        solved[column] = partial / rows[column][column]
    return solved


def kernel(
    nx, ny, cx, cy, nz, cap, wells, direct,
    res_h, acc_h, mob_h, perm_h, near_h, far_h, tr_h, wc_h, wr_h,
    upd_o, out_o,
    res_v, acc_v, mob_v, perm_v, own_idx, nbr_idx, trans,
    wc_ref, wr_ref,
    ps, py, px_l, px_u,
    tot, inv, mix, w_v, ys, flux, offs,
    send_y, recv_y, send_e, send_w, recv_w, recv_e,
    z_own, z_nbr, m_own, m_nbr,
    red_y, red_x,
    load_sem, s0, r0, s1, r1, sy, ry, sx, rx,
):
    gx, gy = lax.axis_index("gx"), lax.axis_index("gy")
    odd = lax.rem(gy, 2)
    beyond = [gy + 1 - 2 * odd, gy - 1 + 2 * odd]
    has_y = [jnp.logical_and(b >= 0, b < ny) for b in beyond]
    upper = [1 - odd, odd]
    base = [(cy - 2) * u for u in upper]
    other_base = [(cy - 2) * (1 - u) for u in upper]
    edge = [(cy - 1) * u for u in upper]
    above, below = odd, 1 - odd
    has_w, has_e = gx > 0, gx < nx - 1

    loads = []
    for k, (src, dst) in enumerate([
        (perm_h, perm_v), (near_h, own_idx.at[above]), (far_h, own_idx.at[below]), (tr_h, trans.at[below]),
        (acc_h, acc_v), (mob_h, mob_v), (res_h, res_v),
        (wc_h, wc_ref), (wr_h, wr_ref),
    ]):
        copy = pltpu.make_async_copy(src, dst, load_sem.at[k])
        copy.start()
        loads.append(copy)

    barrier = pltpu.get_barrier_semaphore()
    for d in range(1, ny):
        pl.semaphore_signal(barrier, inc=1, device_id={"gy": lax.rem(gy + d, ny)}, device_id_type=MESH)
    if direct:
        for flag, other in ((has_w, gx - 1), (has_e, gx + 1)):
            @pl.when(flag)
            def _(other=other):
                pl.semaphore_signal(barrier, inc=1, device_id={"gx": other}, device_id_type=MESH)
        greeted = ny - 1 + has_w.astype(jnp.int32) + has_e.astype(jnp.int32)
    else:
        for d in range(1, nx):
            pl.semaphore_signal(barrier, inc=1, device_id={"gx": lax.rem(gx + d, nx)}, device_id_type=MESH)
        greeted = nx + ny - 2

    loads[0].wait()
    perm = perm_v.reshape(3 * cx * cy, nz)
    for p in range(2):
        ps[p] = perm[pl.ds(cx * cy + edge[p], cx, stride=cy), :]
    for k in (1, 2, 3):
        loads[k].wait()

    pl.semaphore_wait(barrier, greeted)

    def remote(src, dst, send, recv, target):
        return pltpu.make_async_remote_copy(
            src_ref=src, dst_ref=dst, send_sem=send, recv_sem=recv,
            device_id=target, device_id_type=MESH,
        )

    east, west = {"gx": gx + 1}, {"gx": gx - 1}
    across_y = [{"gy": b} for b in beyond]
    has_far = [jnp.logical_and(h, u == 0) for h, u in zip(has_y, upper)]
    has_near = [jnp.logical_and(h, u == 1) for h, u in zip(has_y, upper)]

    first_y = [
        [
            (has_y[p], has_y[p], remote(own_idx.at[p], nbr_idx.at[p], s0.at[p, 0], r0.at[p, 0], across_y[p])),
            (has_y[p], has_y[p], remote(ps.at[p], py.at[p], s0.at[p, 1], r0.at[p, 1], across_y[p])),
            (has_far[p], has_near[p], remote(trans.at[p], trans.at[p], s0.at[p, 2], r0.at[p, 2], across_y[p])),
        ]
        for p in range(2)
    ]
    first_x = [
        (has_e, has_w, remote(perm_v.at[0, cx - 1], px_l, s0.at[2, 0], r0.at[2, 0], east)),
        (has_w, has_e, remote(perm_v.at[0, 0], px_u, s0.at[2, 1], r0.at[2, 1], west)),
    ]

    def start(group):
        for flag, _, copy in group:
            @pl.when(flag)
            def _(copy=copy):
                copy.start()

    def arrive(group):
        for _, flag, copy in group:
            @pl.when(flag)
            def _(copy=copy):
                copy.wait_recv()

    def sent(group):
        for flag, _, copy in group:
            @pl.when(flag)
            def _(copy=copy):
                copy.wait_send()

    def clear(flag, *refs):
        @pl.when(flag)
        def _():
            for ref in refs:
                ref[...] = jnp.zeros(ref.shape, ref.dtype)

    start(first_y[1] + first_x + first_y[0])

    for p in range(2):
        alone = jnp.logical_not(has_y[p])
        clear(alone, nbr_idx.at[p], py.at[p], recv_y.at[p])
        clear(jnp.logical_and(alone, upper[p] == 1), trans.at[p])
    clear(jnp.logical_not(has_w), px_l, recv_w)
    clear(jnp.logical_not(has_e), px_u, recv_e)

    rows = 2 * cx
    row_iota = lax.broadcasted_iota(jnp.int32, (rows, cap), 0)
    layer_iota = lax.broadcasted_iota(jnp.int32, (nz, cap), 0)

    def slots(ref, start_row, onehot, mask):
        index = ref[...]
        column = quotient(index, nz)
        layer = index - column * nz
        across = quotient(column, cy)
        along = column - across * cy - start_row
        hot = jnp.where(layer_iota == layer, 1.0, 0.0).astype(jnp.bfloat16)
        onehot[...] = hot
        mask[...] = jnp.where(row_iota == along * cx + across, 1.0, 0.0).astype(mask.dtype)

    for p in range(2):
        slots(own_idx.at[p], base[p], z_own.at[p], m_own.at[p])

    def scatter(values, mask, onehot):
        parts = []
        for value in values:
            parts.extend(mask[...] * half for half in split_two(value))
        spread = lax.dot_general(
            jnp.concatenate(parts, axis=0), onehot[...], (((1,), (1,)), ((), ())),
            preferred_element_type=jnp.float32,
        )
        return [
            spread[2 * c * rows:(2 * c + 1) * rows] + spread[(2 * c + 1) * rows:(2 * c + 2) * rows]
            for c in range(len(values))
        ]

    def gather(block, mask, onehot):
        found = lax.dot_general(
            jnp.concatenate(split_two(block), axis=0), onehot[...], (((1,), (0,)), ((), ())),
            preferred_element_type=jnp.float32,
        )
        found = found[:3 * rows] + found[3 * rows:]
        return [
            jnp.sum(mask[...] * found[c * rows:(c + 1) * rows], axis=0, keepdims=True)
            for c in range(3)
        ]

    perm_x, perm_y, perm_z = perm_v[0], perm_v[1], perm_v[2]
    y_iota = lax.broadcasted_iota(jnp.int32, (cx, cy, nz), 1)
    z_iota = lax.broadcasted_iota(jnp.int32, (cx, cy, nz), 2)
    t_x = harmonic(perm_x[:-1], perm_x[1:])
    t_n = jnp.where(y_iota == cy - 1, 0.0, harmonic(perm_y, pltpu.roll(perm_y, cy - 1, 1)))
    t_s = jnp.where(y_iota == 0, 0.0, harmonic(perm_y, pltpu.roll(perm_y, 1, 1)))
    t_a = jnp.where(z_iota == nz - 1, 0.0, harmonic(perm_z, pltpu.roll(perm_z, nz - 1, 2)))
    t_b = jnp.where(z_iota == 0, 0.0, harmonic(perm_z, pltpu.roll(perm_z, 1, 2)))

    for k in range(4, 9):
        loads[k].wait()
    lin = (
        lax.broadcasted_iota(jnp.int32, (cx, cy, nz), 0) * (cy * nz) + y_iota * nz + z_iota
    )
    rhs0, rhs1, rhs2 = -res_v[0], -res_v[1], -res_v[2]
    for w in range(wells):
        rhs1 = rhs1 + jnp.where(lin == wc_ref[0, w], wr_ref[0, w], 0.0)
    arrive(first_x)
    t_w0 = harmonic(perm_x[0], px_l[...])
    t_e1 = harmonic(perm_x[cx - 1], px_u[...])
    t_e = jnp.concatenate([t_x, t_e1[None]], axis=0)
    t_w = jnp.concatenate([t_w0[None], t_x], axis=0)

    flat = cx * cy
    tot[...] = (t_e + t_w + t_n + t_s + t_a + t_b).reshape(flat, nz)

    def add_rows(ref, start_row, value):
        place = (pl.ds(start_row, cx, stride=cy), slice(None))
        ref[place] = ref[place] + value

    t_edge = []
    for p in range(2):
        arrive(first_y[p])
        fault_sum = scatter([trans[p]], m_own.at[p], z_own.at[p])[0]
        t_edge.append(harmonic(ps[p], py[p]))
        add_rows(tot, base[p], fault_sum[:cx])
        add_rows(tot, base[p] + 1, fault_sum[cx:])
        add_rows(tot, edge[p], t_edge[p])

    total = tot[...].reshape(cx, cy, nz)
    mob = [[mob_v[a, b] for b in range(3)] for a in range(3)]
    diag = [[acc_v[a, b] + total * mob[a][b] for b in range(3)] for a in range(3)]
    w1 = diag[0][1] / diag[1][1]
    w2 = diag[0][2] / diag[2][2]
    w_v[0] = w1
    w_v[1] = w2
    blk = [[diag[0][b] - w1 * diag[1][b] - w2 * diag[2][b] for b in range(3)], diag[1], diag[2]]

    def part(a, b, c, d):
        return blk[a][b] * blk[c][d] - blk[a][d] * blk[c][b]

    cof = [
        [part(1, 1, 2, 2), -part(1, 0, 2, 2), part(1, 0, 2, 1)],
        [-part(0, 1, 2, 2), part(0, 0, 2, 2), -part(0, 0, 2, 1)],
        [part(0, 1, 1, 2), -part(0, 0, 1, 2), part(0, 0, 1, 1)],
    ]
    det = blk[0][0] * cof[0][0] + blk[0][1] * cof[0][1] + blk[0][2] * cof[0][2]
    inverse_det = 1.0 / det
    pre = [[cof[b][a] * inverse_det for b in range(3)] for a in range(3)]
    for a in range(3):
        for b in range(3):
            inv[a, b] = pre[a][b]
            mix[a, b] = mob[a][0] * pre[0][b] + mob[a][1] * pre[1][b] + mob[a][2] * pre[2][b]

    ys[0, 0] = rhs0 - w1 * rhs1 - w2 * rhs2
    ys[0, 1] = rhs1
    ys[0, 2] = rhs2

    def product(left, right):
        return jnp.sum(jnp.sum(ys[left] * ys[right], axis=(0, 1)), axis=0, keepdims=True)

    pending = first_x + first_y[0] + first_y[1]
    for it in range(KRYLOV):
        y = [ys[it, c] for c in range(3)]
        field = []
        for a in range(3):
            value = mix[a, 0] * y[0] + mix[a, 1] * y[1] + mix[a, 2] * y[2]
            field.append(value)
            flux[pl.ds(a * flat, flat), :] = value.reshape(flat, nz)
            send_e[it, a] = value[cx - 1]
            send_w[it, a] = value[0]
        for p in (1, 0):
            for a in range(3):
                for r in range(2):
                    send_y[p, it, pl.ds((2 * a + r) * cx, cx), :] = flux[pl.ds(a * flat + base[p] + r, cx, stride=cy), :]
        copies_y = [
            [(has_y[p], has_y[p], remote(send_y.at[p, it], recv_y.at[p, it], s1.at[it, p], r1.at[it, p], across_y[p]))]
            for p in range(2)
        ]
        copies_x = [
            (has_e, has_w, remote(send_e.at[it], recv_w.at[it], s1.at[it, 2], r1.at[it, 2], east)),
            (has_w, has_e, remote(send_w.at[it], recv_e.at[it], s1.at[it, 3], r1.at[it, 3], west)),
        ]
        start(copies_y[1] + copies_x + copies_y[0])
        pending += copies_x + copies_y[0] + copies_y[1]
        if it == 0:
            for p in range(2):
                slots(nbr_idx.at[p], other_base[p], z_nbr.at[p], m_nbr.at[p])
        inner = []
        for a in range(3):
            f = field[a]
            near_sums = (
                t_n * pltpu.roll(f, cy - 1, 1) + t_s * pltpu.roll(f, 1, 1)
                + t_a * pltpu.roll(f, nz - 1, 2) + t_b * pltpu.roll(f, 1, 2)
            )
            inner.append(near_sums)
        if it == KRYLOV - 1:
            rows_early = [product(left, right) for left, right in PAIRS if right < KRYLOV]
        arrive(copies_x)
        for a in range(3):
            f = field[a]
            value = (
                inner[a]
                + t_e * jnp.concatenate([f[1:], recv_e[it, a][None]], axis=0)
                + t_w * jnp.concatenate([recv_w[it, a][None], f[:-1]], axis=0)
            )
            offs[pl.ds(a * flat, flat), :] = value.reshape(flat, nz)
        for p in range(2):
            arrive(copies_y[p])
            got = gather(recv_y[p, it], m_nbr.at[p], z_nbr.at[p])
            fault = scatter([trans[p] * g for g in got], m_own.at[p], z_own.at[p])
            for a in range(3):
                at = pl.multiple_of((2 * a + 1 - upper[p]) * cx, cx)
                halo = recv_y[p, it, pl.ds(at, cx), :]
                add_rows(offs, a * flat + base[p], fault[a][:cx])
                add_rows(offs, a * flat + base[p] + 1, fault[a][cx:])
                add_rows(offs, a * flat + edge[p], t_edge[p] * halo)
        o = [offs[pl.ds(a * flat, flat), :].reshape(cx, cy, nz) for a in range(3)]
        ys[it + 1, 0] = o[0] - w_v[0] * o[1] - w_v[1] * o[2]
        ys[it + 1, 1] = o[1]
        ys[it + 1, 2] = o[2]

    rows_late = [product(left, KRYLOV) for left in range(KRYLOV + 1)]
    count = -(-len(PAIRS) // 8) * 8
    blank = jnp.zeros((count - len(PAIRS), nz), jnp.float32)
    table = jnp.concatenate(rows_early + rows_late + [blank], axis=0)
    on_lane = (
        lax.broadcasted_iota(jnp.int32, (count, nz), 0)
        == lax.broadcasted_iota(jnp.int32, (count, nz), 1)
    )

    def to_lanes(block):
        filled = jnp.broadcast_to(jnp.sum(block, axis=1, keepdims=True), block.shape)
        return jnp.sum(jnp.where(on_lane, filled, 0.0), axis=0, keepdims=True)

    def total_of(ref, size):
        value = ref[0]
        for d in range(1, size):
            value = value + ref[d]
        return value

    line = to_lanes(table)
    shared = []
    if direct:
        me = gx * ny + gy
        red_y[me] = line
        for dx in range(nx):
            for dy in range(ny):
                if dx or dy:
                    k = dx * ny + dy
                    target = {"gx": lax.rem(gx + dx, nx), "gy": lax.rem(gy + dy, ny)}
                    shared.append(remote(red_y.at[me], red_y.at[me], sy.at[k], ry.at[k], target))
        for copy in shared:
            copy.start()
        for copy in shared:
            copy.wait_recv()
        line = total_of(red_y, nx * ny)
    else:
        for axis, me, size, ref, send, recv in (
            ("gy", gy, ny, red_y, sy, ry), ("gx", gx, nx, red_x, sx, rx),
        ):
            ref[me] = line
            stage = [
                remote(ref.at[me], ref.at[me], send.at[d], recv.at[d], {axis: lax.rem(me + d, size)})
                for d in range(1, size)
            ]
            for copy in stage:
                copy.start()
            for copy in stage:
                copy.wait_recv()
            shared.extend(stage)
            line = total_of(ref, size)
    spread = jnp.where(on_lane, jnp.broadcast_to(line, (count, nz)), 0.0)
    sums = jnp.broadcast_to(jnp.sum(spread, axis=1, keepdims=True), (count, nz))

    def entry(left, right):
        k = PAIRS.index((min(left, right), max(left, right)))
        return sums[k:k + 1]

    normal = [
        [(entry(a, b) - entry(a, b + 1)) - (entry(a + 1, b) - entry(a + 1, b + 1)) for b in range(KRYLOV)]
        for a in range(KRYLOV)
    ]
    coefs = solve_small(normal, [entry(0, a) - entry(0, a + 1) for a in range(KRYLOV)])
    left_over = [1.0 - coefs[0]] + [coefs[k] - coefs[k + 1] for k in range(KRYLOV - 1)] + [coefs[-1]]
    coefs = [c.reshape(1, 1, nz) for c in coefs]
    left_over = [c.reshape(1, 1, nz) for c in left_over]
    mixed = []
    for c in range(3):
        combined = coefs[0] * ys[0, c]
        rest = left_over[0] * ys[0, c]
        for k in range(1, KRYLOV):
            combined = combined + coefs[k] * ys[k, c]
            rest = rest + left_over[k] * ys[k, c]
        mixed.append(combined)
        out_o[c] = rest + left_over[KRYLOV] * ys[KRYLOV, c]
    for c in range(3):
        upd_o[c] = inv[c, 0] * mixed[0] + inv[c, 1] * mixed[1] + inv[c, 2] * mixed[2]
    sent(pending)
    for copy in shared:
        copy.wait_send()


def put_out(update_v, rest_v, update_h, rest_h, sem):
    copies = [
        pltpu.make_async_copy(update_v, update_h, sem.at[0]),
        pltpu.make_async_copy(rest_v, rest_h, sem.at[1]),
    ]
    for copy in copies:
        copy.start()
    for copy in copies:
        copy.wait()


def solution(mesh):
    nx, ny = mesh.shape["gx"], mesh.shape["gy"]
    placed = (
        P(None, "gx", "gy", None),
        P(None, None, "gx", "gy", None),
        P(None, None, "gx", "gy", None),
        P(None, "gx", "gy", None),
    ) + (P("gx", "gy", None),) * 5

    def shards(residual_in, accumulation, mobility, permeability, fault_near, fault_far, fault_trans, well_cells, well_rates):
        _, cx, cy, nz = residual_in.shape
        cap = fault_near.shape[-1]
        wells = well_cells.shape[-1]
        flat = cx * cy
        direct = nx <= KRYLOV + 2 and nx * ny <= 64
        stages = (nx * ny if direct else ny, nx)
        f32, i32, bf16 = jnp.float32, jnp.int32, jnp.bfloat16
        vm = pltpu.VMEM
        dma = pltpu.SemaphoreType.DMA
        scratch = [
            vm((3, cx, cy, nz), f32), vm((3, 3, cx, cy, nz), f32), vm((3, 3, cx, cy, nz), f32),
            vm((3, cx, cy, nz), f32),
            vm((2, 1, cap), i32), vm((2, 1, cap), i32), vm((2, 1, cap), f32),
            pltpu.SMEM((1, wells), i32), pltpu.SMEM((1, wells), f32),
        ]
        scratch += [vm((2, cx, nz), f32)] * 2 + [vm((cy, nz), f32)] * 2
        scratch += [
            vm((flat, nz), f32), vm((3, 3, cx, cy, nz), f32), vm((3, 3, cx, cy, nz), f32),
            vm((2, cx, cy, nz), f32), vm((KRYLOV + 1, 3, cx, cy, nz), f32),
            vm((3 * flat, nz), f32), vm((3 * flat, nz), f32),
        ]
        scratch += [vm((2, KRYLOV, 6 * cx, nz), f32)] * 2 + [vm((KRYLOV, 3, cy, nz), f32)] * 4
        scratch += [vm((2, nz, cap), bf16)] * 2 + [vm((2, 2 * cx, cap), bf16), vm((2, 2 * cx, cap), f32)]
        scratch += [vm((stages[0], 1, nz), f32), vm((stages[1], 1, nz), f32)]
        scratch += [
            dma((9,)), dma((3, 3)), dma((3, 3)), dma((KRYLOV, 4)), dma((KRYLOV, 4)),
            dma((stages[0],)), dma((stages[0],)), dma((stages[1],)), dma((stages[1],)),
        ]
        anywhere = pl.BlockSpec(memory_space=pl.ANY)
        inside = pl.BlockSpec(memory_space=pltpu.VMEM)
        held = pltpu.VMEM(residual_in.shape, f32)
        shape = jax.ShapeDtypeStruct(residual_in.shape, f32)
        update, rest = pl.pallas_call(
            functools.partial(kernel, nx, ny, cx, cy, nz, cap, wells, direct),
            out_shape=(held, held),
            in_specs=[anywhere] * 9,
            out_specs=(inside, inside),
            scratch_shapes=scratch,
            compiler_params=pltpu.CompilerParams(collective_id=0, has_side_effects=True),
            name="newton",
        )(
            residual_in, accumulation, mobility, permeability,
            fault_near.reshape(1, cap), fault_far.reshape(1, cap), fault_trans.reshape(1, cap),
            well_cells.reshape(1, wells), well_rates.reshape(1, wells),
        )
        return pl.pallas_call(
            put_out,
            out_shape=(shape, shape),
            in_specs=[anywhere] * 2,
            out_specs=(anywhere, anywhere),
            scratch_shapes=[dma((2,))],
            compiler_params=pltpu.CompilerParams(vmem_limit_bytes=1 << 20),
            name="put_out",
        )(*(pltpu.with_memory_space_constraint(v, pltpu.MemorySpace.VMEM) for v in (update, rest)))

    out = P(None, "gx", "gy", None)
    return jax.shard_map(shards, mesh=mesh, in_specs=placed, out_specs=(out, out), check_vma=False)
```

```python
import functools

import jax
import jax.numpy as jnp
from jax import lax
from jax.experimental import pallas as pl
from jax.experimental.pallas import tpu as pltpu
from jax.sharding import PartitionSpec as P

KRYLOV = 3
PAIRS = [(a, b) for b in range(KRYLOV + 1) for a in range(b + 1)]
MESH = pl.DeviceIdType.MESH


def harmonic(a, b):
    return 2.0 * a * b / (a + b)


def quotient(value, by):
    if by & (by - 1) == 0:
        return lax.shift_right_logical(value, jnp.int32(by.bit_length() - 1))
    return value // by


def split_two(value):
    high = value.astype(jnp.bfloat16)
    low = (value - high.astype(jnp.float32)).astype(jnp.bfloat16)
    return high, low


def solve_small(matrix, rhs_values):
    size = len(rhs_values)
    rows = [list(line) for line in matrix]
    values = list(rhs_values)
    for column in range(size):
        for lower in range(column + 1, size):
            factor = rows[lower][column] / rows[column][column]
            rows[lower] = [e - factor * p for e, p in zip(rows[lower], rows[column])]
            values[lower] = values[lower] - factor * values[column]
    solved = [0.0] * size
    for column in reversed(range(size)):
        partial = values[column]
        for later in range(column + 1, size):
            partial = partial - rows[column][later] * solved[later]
        solved[column] = partial / rows[column][column]
    return solved


def kernel(
    nx, ny, cx, cy, nz, cap, wells, direct,
    res_h, acc_h, mob_h, perm_h, near_h, far_h, tr_h, wc_h, wr_h,
    upd_o, out_o,
    res_v, acc_v, mob_v, perm_v, near_v, far_v, tr_v,
    wc_ref, wr_ref,
    far_u, tr_u, near_l,
    ps_u, ps_l, py_l, py_u, px_l, px_u,
    tot, inv, mix, w_v, ys, flux, offs,
    send_u, send_l, send_e, send_w, recv_l, recv_u, recv_w, recv_e,
    z_far, z_near, z_near_l, z_far_u,
    m_far, m_near, m_near_l, m_far_u,
    red_y, red_x,
    load_sem, s0, r0, s1, r1, sy, ry, sx, rx,
):
    gx, gy = lax.axis_index("gx"), lax.axis_index("gy")
    has_l, has_u = gy > 0, gy < ny - 1
    has_w, has_e = gx > 0, gx < nx - 1

    loads = []
    for k, (src, dst) in enumerate([
        (perm_h, perm_v), (near_h, near_v), (far_h, far_v), (tr_h, tr_v),
        (acc_h, acc_v), (mob_h, mob_v), (res_h, res_v),
        (wc_h, wc_ref), (wr_h, wr_ref),
    ]):
        copy = pltpu.make_async_copy(src, dst, load_sem.at[k])
        copy.start()
        loads.append(copy)

    barrier = pltpu.get_barrier_semaphore()
    for d in range(1, ny):
        pl.semaphore_signal(barrier, inc=1, device_id={"gy": lax.rem(gy + d, ny)}, device_id_type=MESH)
    if direct:
        for flag, other in ((has_w, gx - 1), (has_e, gx + 1)):
            @pl.when(flag)
            def _(other=other):
                pl.semaphore_signal(barrier, inc=1, device_id={"gx": other}, device_id_type=MESH)
        greeted = ny - 1 + has_w.astype(jnp.int32) + has_e.astype(jnp.int32)
    else:
        for d in range(1, nx):
            pl.semaphore_signal(barrier, inc=1, device_id={"gx": lax.rem(gx + d, nx)}, device_id_type=MESH)
        greeted = nx + ny - 2

    loads[0].wait()
    perm = perm_v.reshape(3 * cx * cy, nz)
    ps_u[...] = perm[pl.ds(cx * cy + cy - 1, cx, stride=cy), :]
    ps_l[...] = perm[pl.ds(cx * cy, cx, stride=cy), :]
    for k in (1, 2, 3):
        loads[k].wait()

    pl.semaphore_wait(barrier, greeted)

    def remote(src, dst, send, recv, target):
        return pltpu.make_async_remote_copy(
            src_ref=src, dst_ref=dst, send_sem=send, recv_sem=recv,
            device_id=target, device_id_type=MESH,
        )

    up, down = {"gy": gy + 1}, {"gy": gy - 1}
    east, west = {"gx": gx + 1}, {"gx": gx - 1}
    first_u = [
        remote(near_v, near_l, s0.at[0], r0.at[0], up),
        remote(ps_u, py_l, s0.at[1], r0.at[1], up),
    ]
    first_l = [
        remote(far_v, far_u, s0.at[2], r0.at[2], down),
        remote(tr_v, tr_u, s0.at[3], r0.at[3], down),
        remote(ps_l, py_u, s0.at[4], r0.at[4], down),
    ]
    first_e = [remote(perm_v.at[0, cx - 1], px_l, s0.at[5], r0.at[5], east)]
    first_w = [remote(perm_v.at[0, 0], px_u, s0.at[6], r0.at[6], west)]

    def start(to_u, to_l, to_e, to_w):
        for flag, copies in ((has_u, to_u), (has_l, to_l), (has_e, to_e), (has_w, to_w)):
            @pl.when(flag)
            def _(copies=copies):
                for copy in copies:
                    copy.start()

    def arrive(to_u, to_l, to_e, to_w):
        for flag, copies in ((has_u, to_l), (has_l, to_u), (has_e, to_w), (has_w, to_e)):
            @pl.when(flag)
            def _(copies=copies):
                for copy in copies:
                    copy.wait_recv()

    def sent(to_u, to_l, to_e, to_w):
        for flag, copies in ((has_u, to_u), (has_l, to_l), (has_e, to_e), (has_w, to_w)):
            @pl.when(flag)
            def _(copies=copies):
                for copy in copies:
                    copy.wait_send()

    start(first_u, first_l, first_e, first_w)

    def clear(flag, *refs):
        @pl.when(jnp.logical_not(flag))
        def _():
            for ref in refs:
                ref[...] = jnp.zeros(ref.shape, ref.dtype)

    clear(has_l, near_l, py_l, recv_l)
    clear(has_u, far_u, tr_u, py_u, recv_u)
    clear(has_w, px_l, recv_w)
    clear(has_e, px_u, recv_e)

    rows = 2 * cx
    row_iota = lax.broadcasted_iota(jnp.int32, (rows, cap), 0)
    layer_iota = lax.broadcasted_iota(jnp.int32, (nz, cap), 0)

    def slots(ref, base, onehot, mask):
        index = ref[...]
        column = quotient(index, nz)
        layer = index - column * nz
        across = quotient(column, cy)
        along = column - across * cy - base
        hot = jnp.where(layer_iota == layer, 1.0, 0.0).astype(jnp.bfloat16)
        for copy in range(onehot.shape[0] // nz):
            onehot[pl.ds(copy * nz, nz), :] = hot
        mask[...] = jnp.where(row_iota == along * cx + across, 1.0, 0.0).astype(mask.dtype)

    slots(far_v, 0, z_far, m_far)
    slots(near_v, cy - 2, z_near, m_near)

    def scatter(values, mask, onehot):
        parts = []
        for value in values:
            parts.extend(mask[...] * half for half in split_two(value))
        spread = lax.dot_general(
            jnp.concatenate(parts, axis=0), onehot[...], (((1,), (1,)), ((), ())),
            preferred_element_type=jnp.float32,
        )
        return [
            spread[2 * c * rows:(2 * c + 1) * rows] + spread[(2 * c + 1) * rows:(2 * c + 2) * rows]
            for c in range(len(values))
        ]

    def gather(block, mask, onehot):
        found = lax.dot_general(
            jnp.concatenate(split_two(block), axis=0), onehot[...], (((1,), (0,)), ((), ())),
            preferred_element_type=jnp.float32,
        )
        found = found[:3 * rows] + found[3 * rows:]
        return [
            jnp.sum(mask[...] * found[c * rows:(c + 1) * rows], axis=0, keepdims=True)
            for c in range(3)
        ]

    trans = tr_v[...]
    perm_x, perm_y, perm_z = perm_v[0], perm_v[1], perm_v[2]
    y_iota = lax.broadcasted_iota(jnp.int32, (cx, cy, nz), 1)
    z_iota = lax.broadcasted_iota(jnp.int32, (cx, cy, nz), 2)
    t_x = harmonic(perm_x[:-1], perm_x[1:])
    t_n = jnp.where(y_iota == cy - 1, 0.0, harmonic(perm_y, pltpu.roll(perm_y, cy - 1, 1)))
    t_s = jnp.where(y_iota == 0, 0.0, harmonic(perm_y, pltpu.roll(perm_y, 1, 1)))
    t_a = jnp.where(z_iota == nz - 1, 0.0, harmonic(perm_z, pltpu.roll(perm_z, nz - 1, 2)))
    t_b = jnp.where(z_iota == 0, 0.0, harmonic(perm_z, pltpu.roll(perm_z, 1, 2)))
    far_sum = scatter([trans], m_far, z_far)[0]

    for k in range(4, 9):
        loads[k].wait()
    lin = (
        lax.broadcasted_iota(jnp.int32, (cx, cy, nz), 0) * (cy * nz) + y_iota * nz + z_iota
    )
    rhs0, rhs1, rhs2 = -res_v[0], -res_v[1], -res_v[2]
    for w in range(wells):
        rhs1 = rhs1 + jnp.where(lin == wc_ref[0, w], wr_ref[0, w], 0.0)
    arrive(first_u, first_l, first_e, first_w)
    trans_u = tr_u[...]
    near_sum = scatter([trans_u], m_near, z_near)[0]
    t_w0 = harmonic(perm_x[0], px_l[...])
    t_e1 = harmonic(perm_x[cx - 1], px_u[...])
    t_e = jnp.concatenate([t_x, t_e1[None]], axis=0)
    t_w = jnp.concatenate([t_w0[None], t_x], axis=0)
    t_s0 = harmonic(ps_l[...], py_l[...])
    t_n1 = harmonic(ps_u[...], py_u[...])

    flat = cx * cy
    tot[...] = (t_e + t_w + t_n + t_s + t_a + t_b).reshape(flat, nz)

    def add_rows(ref, start_row, value):
        place = (pl.ds(start_row, cx, stride=cy), slice(None))
        ref[place] = ref[place] + value

    add_rows(tot, 0, far_sum[:cx] + t_s0)
    add_rows(tot, 1, far_sum[cx:])
    add_rows(tot, cy - 2, near_sum[:cx])
    add_rows(tot, cy - 1, near_sum[cx:] + t_n1)

    total = tot[...].reshape(cx, cy, nz)
    mob = [[mob_v[a, b] for b in range(3)] for a in range(3)]
    diag = [[acc_v[a, b] + total * mob[a][b] for b in range(3)] for a in range(3)]
    w1 = diag[0][1] / diag[1][1]
    w2 = diag[0][2] / diag[2][2]
    w_v[0] = w1
    w_v[1] = w2
    blk = [[diag[0][b] - w1 * diag[1][b] - w2 * diag[2][b] for b in range(3)], diag[1], diag[2]]

    def part(a, b, c, d):
        return blk[a][b] * blk[c][d] - blk[a][d] * blk[c][b]

    cof = [
        [part(1, 1, 2, 2), -part(1, 0, 2, 2), part(1, 0, 2, 1)],
        [-part(0, 1, 2, 2), part(0, 0, 2, 2), -part(0, 0, 2, 1)],
        [part(0, 1, 1, 2), -part(0, 0, 1, 2), part(0, 0, 1, 1)],
    ]
    det = blk[0][0] * cof[0][0] + blk[0][1] * cof[0][1] + blk[0][2] * cof[0][2]
    inverse_det = 1.0 / det
    pre = [[cof[b][a] * inverse_det for b in range(3)] for a in range(3)]
    for a in range(3):
        for b in range(3):
            inv[a, b] = pre[a][b]
            mix[a, b] = mob[a][0] * pre[0][b] + mob[a][1] * pre[1][b] + mob[a][2] * pre[2][b]

    ys[0, 0] = rhs0 - w1 * rhs1 - w2 * rhs2
    ys[0, 1] = rhs1
    ys[0, 2] = rhs2

    def product(left, right):
        return jnp.sum(jnp.sum(ys[left] * ys[right], axis=(0, 1)), axis=0, keepdims=True)

    pending = [(first_u, first_l, first_e, first_w)]
    for it in range(KRYLOV):
        y = [ys[it, c] for c in range(3)]
        field = []
        for a in range(3):
            value = mix[a, 0] * y[0] + mix[a, 1] * y[1] + mix[a, 2] * y[2]
            field.append(value)
            flux[pl.ds(a * flat, flat), :] = value.reshape(flat, nz)
            send_e[it, a] = value[cx - 1]
            send_w[it, a] = value[0]
        for a in range(3):
            for r in range(2):
                at = pl.ds((2 * a + r) * cx, cx)
                send_u[it, at, :] = flux[pl.ds(a * flat + cy - 2 + r, cx, stride=cy), :]
                send_l[it, at, :] = flux[pl.ds(a * flat + r, cx, stride=cy), :]
        copies = (
            [remote(send_u.at[it], recv_l.at[it], s1.at[it, 0], r1.at[it, 0], up)],
            [remote(send_l.at[it], recv_u.at[it], s1.at[it, 1], r1.at[it, 1], down)],
            [remote(send_e.at[it], recv_w.at[it], s1.at[it, 2], r1.at[it, 2], east)],
            [remote(send_w.at[it], recv_e.at[it], s1.at[it, 3], r1.at[it, 3], west)],
        )
        start(*copies)
        pending.append(copies)
        if it == 0:
            slots(near_l, cy - 2, z_near_l, m_near_l)
            slots(far_u, 0, z_far_u, m_far_u)
        inner = []
        for a in range(3):
            f = field[a]
            near_sums = (
                t_n * pltpu.roll(f, cy - 1, 1) + t_s * pltpu.roll(f, 1, 1)
                + t_a * pltpu.roll(f, nz - 1, 2) + t_b * pltpu.roll(f, 1, 2)
            )
            inner.append(near_sums)
        if it == KRYLOV - 1:
            rows_early = [product(left, right) for left, right in PAIRS if right < KRYLOV]
        arrive(*copies)
        below, above = recv_l[it], recv_u[it]
        got_l = gather(below, m_near_l, z_near_l)
        got_u = gather(above, m_far_u, z_far_u)
        fault_l = scatter([trans * g for g in got_l], m_far, z_far)
        fault_u = scatter([trans_u * g for g in got_u], m_near, z_near)
        for a in range(3):
            f = field[a]
            value = (
                inner[a]
                + t_e * jnp.concatenate([f[1:], recv_e[it, a][None]], axis=0)
                + t_w * jnp.concatenate([recv_w[it, a][None], f[:-1]], axis=0)
            )
            offs[pl.ds(a * flat, flat), :] = value.reshape(flat, nz)
            halo_s = below[(2 * a + 1) * cx:(2 * a + 2) * cx]
            halo_n = above[2 * a * cx:(2 * a + 1) * cx]
            add_rows(offs, a * flat, fault_l[a][:cx] + t_s0 * halo_s)
            add_rows(offs, a * flat + 1, fault_l[a][cx:])
            add_rows(offs, a * flat + cy - 2, fault_u[a][:cx])
            add_rows(offs, a * flat + cy - 1, fault_u[a][cx:] + t_n1 * halo_n)
        o = [offs[pl.ds(a * flat, flat), :].reshape(cx, cy, nz) for a in range(3)]
        ys[it + 1, 0] = o[0] - w_v[0] * o[1] - w_v[1] * o[2]
        ys[it + 1, 1] = o[1]
        ys[it + 1, 2] = o[2]

    rows_late = [product(left, KRYLOV) for left in range(KRYLOV + 1)]
    count = -(-len(PAIRS) // 8) * 8
    blank = jnp.zeros((count - len(PAIRS), nz), jnp.float32)
    table = jnp.concatenate(rows_early + rows_late + [blank], axis=0)
    on_lane = (
        lax.broadcasted_iota(jnp.int32, (count, nz), 0)
        == lax.broadcasted_iota(jnp.int32, (count, nz), 1)
    )

    def to_lanes(block):
        filled = jnp.broadcast_to(jnp.sum(block, axis=1, keepdims=True), block.shape)
        return jnp.sum(jnp.where(on_lane, filled, 0.0), axis=0, keepdims=True)

    def total_of(ref, size):
        value = ref[0]
        for d in range(1, size):
            value = value + ref[d]
        return value

    line = to_lanes(table)
    shared = []
    if direct:
        me = gx * ny + gy
        red_y[me] = line
        for dx in range(nx):
            for dy in range(ny):
                if dx or dy:
                    k = dx * ny + dy
                    target = {"gx": lax.rem(gx + dx, nx), "gy": lax.rem(gy + dy, ny)}
                    shared.append(remote(red_y.at[me], red_y.at[me], sy.at[k], ry.at[k], target))
        for copy in shared:
            copy.start()
        for copy in shared:
            copy.wait_recv()
        line = total_of(red_y, nx * ny)
    else:
        for axis, me, size, ref, send, recv in (
            ("gy", gy, ny, red_y, sy, ry), ("gx", gx, nx, red_x, sx, rx),
        ):
            ref[me] = line
            stage = [
                remote(ref.at[me], ref.at[me], send.at[d], recv.at[d], {axis: lax.rem(me + d, size)})
                for d in range(1, size)
            ]
            for copy in stage:
                copy.start()
            for copy in stage:
                copy.wait_recv()
            shared.extend(stage)
            line = total_of(ref, size)
    spread = jnp.where(on_lane, jnp.broadcast_to(line, (count, nz)), 0.0)
    sums = jnp.broadcast_to(jnp.sum(spread, axis=1, keepdims=True), (count, nz))

    def entry(left, right):
        k = PAIRS.index((min(left, right), max(left, right)))
        return sums[k:k + 1]

    normal = [
        [(entry(a, b) - entry(a, b + 1)) - (entry(a + 1, b) - entry(a + 1, b + 1)) for b in range(KRYLOV)]
        for a in range(KRYLOV)
    ]
    coefs = solve_small(normal, [entry(0, a) - entry(0, a + 1) for a in range(KRYLOV)])
    left_over = [1.0 - coefs[0]] + [coefs[k] - coefs[k + 1] for k in range(KRYLOV - 1)] + [coefs[-1]]
    coefs = [c.reshape(1, 1, nz) for c in coefs]
    left_over = [c.reshape(1, 1, nz) for c in left_over]
    mixed = []
    for c in range(3):
        combined = coefs[0] * ys[0, c]
        rest = left_over[0] * ys[0, c]
        for k in range(1, KRYLOV):
            combined = combined + coefs[k] * ys[k, c]
            rest = rest + left_over[k] * ys[k, c]
        mixed.append(combined)
        out_o[c] = rest + left_over[KRYLOV] * ys[KRYLOV, c]
    for c in range(3):
        upd_o[c] = inv[c, 0] * mixed[0] + inv[c, 1] * mixed[1] + inv[c, 2] * mixed[2]
    for group in pending:
        sent(*group)
    for copy in shared:
        copy.wait_send()


def put_out(update_v, rest_v, update_h, rest_h, sem):
    copies = [
        pltpu.make_async_copy(update_v, update_h, sem.at[0]),
        pltpu.make_async_copy(rest_v, rest_h, sem.at[1]),
    ]
    for copy in copies:
        copy.start()
    for copy in copies:
        copy.wait()


def solution(mesh):
    nx, ny = mesh.shape["gx"], mesh.shape["gy"]
    placed = (
        P(None, "gx", "gy", None),
        P(None, None, "gx", "gy", None),
        P(None, None, "gx", "gy", None),
        P(None, "gx", "gy", None),
    ) + (P("gx", "gy", None),) * 5

    def shards(residual_in, accumulation, mobility, permeability, fault_near, fault_far, fault_trans, well_cells, well_rates):
        _, cx, cy, nz = residual_in.shape
        cap = fault_near.shape[-1]
        wells = well_cells.shape[-1]
        flat = cx * cy
        direct = nx <= KRYLOV + 2 and nx * ny <= 64
        stages = (nx * ny if direct else ny, nx)
        f32, i32, bf16 = jnp.float32, jnp.int32, jnp.bfloat16
        vm = pltpu.VMEM
        dma = pltpu.SemaphoreType.DMA
        scratch = [
            vm((3, cx, cy, nz), f32), vm((3, 3, cx, cy, nz), f32), vm((3, 3, cx, cy, nz), f32),
            vm((3, cx, cy, nz), f32),
            vm((1, cap), i32), vm((1, cap), i32), vm((1, cap), f32),
            pltpu.SMEM((1, wells), i32), pltpu.SMEM((1, wells), f32),
            vm((1, cap), i32), vm((1, cap), f32), vm((1, cap), i32),
        ]
        scratch += [vm((cx, nz), f32)] * 4 + [vm((cy, nz), f32)] * 2
        scratch += [
            vm((flat, nz), f32), vm((3, 3, cx, cy, nz), f32), vm((3, 3, cx, cy, nz), f32),
            vm((2, cx, cy, nz), f32), vm((KRYLOV + 1, 3, cx, cy, nz), f32),
            vm((3 * flat, nz), f32), vm((3 * flat, nz), f32),
        ]
        scratch += [vm((KRYLOV, 6 * cx, nz), f32)] * 2 + [vm((KRYLOV, 3, cy, nz), f32)] * 2
        scratch += [vm((KRYLOV, 6 * cx, nz), f32)] * 2 + [vm((KRYLOV, 3, cy, nz), f32)] * 2
        scratch += [vm((nz, cap), bf16)] * 4
        scratch += [vm((2 * cx, cap), bf16)] * 2 + [vm((2 * cx, cap), f32)] * 2
        scratch += [vm((stages[0], 1, nz), f32), vm((stages[1], 1, nz), f32)]
        scratch += [
            dma((9,)), dma((7,)), dma((7,)), dma((KRYLOV, 4)), dma((KRYLOV, 4)),
            dma((stages[0],)), dma((stages[0],)), dma((stages[1],)), dma((stages[1],)),
        ]
        anywhere = pl.BlockSpec(memory_space=pl.ANY)
        inside = pl.BlockSpec(memory_space=pltpu.VMEM)
        held = pltpu.VMEM(residual_in.shape, f32)
        shape = jax.ShapeDtypeStruct(residual_in.shape, f32)
        update, rest = pl.pallas_call(
            functools.partial(kernel, nx, ny, cx, cy, nz, cap, wells, direct),
            out_shape=(held, held),
            in_specs=[anywhere] * 9,
            out_specs=(inside, inside),
            scratch_shapes=scratch,
            compiler_params=pltpu.CompilerParams(collective_id=0, has_side_effects=True),
            name="newton",
        )(
            residual_in, accumulation, mobility, permeability,
            fault_near.reshape(1, cap), fault_far.reshape(1, cap), fault_trans.reshape(1, cap),
            well_cells.reshape(1, wells), well_rates.reshape(1, wells),
        )
        return pl.pallas_call(
            put_out,
            out_shape=(shape, shape),
            in_specs=[anywhere] * 2,
            out_specs=(anywhere, anywhere),
            scratch_shapes=[dma((2,))],
            compiler_params=pltpu.CompilerParams(vmem_limit_bytes=1 << 20),
            name="put_out",
        )(*(pltpu.with_memory_space_constraint(v, pltpu.MemorySpace.VMEM) for v in (update, rest)))

    out = P(None, "gx", "gy", None)
    return jax.shard_map(shards, mesh=mesh, in_specs=placed, out_specs=(out, out), check_vma=False)
```
